32 devices in a mesh: parts: 2 (over y), genome: 8 (over z, x), sample: 2 (over core).
Axes of the slice: x: 2, y: 2, z: 4, core: 2. Of those that a mesh axis runs over, the one named last changes fastest.
Arguments:
- signal: bfloat16 [768, 32768], P('sample', ('parts', 'genome')), parts along dimension 1, may hold values from -740 to 740
- coverage: int32 [768, 32768], P('sample', ('parts', 'genome')), parts along dimension 1, may hold values 0 or 1
- design_codes: int32 [7, 768], P(None, 'sample'), may hold values from 0 to 4
- level_prior: float32 [11], replicated, may hold values from 0.1 to 10
Outputs:
- effect_tracks: float32 [8, 32768], P('sample', ('parts', 'genome')), parts along dimension 1
The draws below stay inside these ranges and needn't reach their ends.
There are 2 independent parts, one for each index of `parts`. The reference program is written for one: setup_inputs(seed, part) draws one part's arguments, and reference() takes and returns one part's arrays. A program takes and returns all parts, laid end to end along the dimension named above; an argument that names none is the same for every part. Nothing has to cross between parts.
All inputs are finite; a program needn't handle non-finite values. No bound on the sum of `coverage` on one device may be relied on, other than what follows from the above.
Results may differ from the reference program's by a relative error of at most 0.0003.
Values sent between devices are 32-bit elements; how exact they have to be, the bound alone decides.
A program may use at most 64 MiB of HBM per device.

```python
import math
import jax
import jax.numpy as jnp
from jax import lax

LEVELS = 10
DESIGN = 8
CODES = 7
SAMPLES = 768
POSITIONS = 16384


def draw_signal(key, part):
    first, second, third = jax.random.split(key, 3)
    values = jnp.clip(jax.random.normal(first, (SAMPLES, POSITIONS), jnp.float32), -6.0, 6.0)
    row_scale = jnp.exp(jax.random.uniform(second, (SAMPLES, 1), jnp.float32, 0.0, math.log(10.0)))
    column_scale = jnp.exp(jax.random.uniform(third, (1, POSITIONS), jnp.float32, 0.0, math.log(10.0)))
    return (values * row_scale * column_scale).astype(jnp.bfloat16)


def touch_ends(result, rng, smallest, largest):
    longest = result.shape.index(max(result.shape))
    spots = []
    for shift in (0, 1):
        where = [jax.random.randint(jax.random.fold_in(rng, axis), (), 0, length) for axis, length in enumerate(result.shape)]
        where[longest] = (where[longest] + shift) % result.shape[longest]
        spots.append(tuple(where))
    return result.at[spots[0]].set(smallest).at[spots[1]].set(largest)


def setup_inputs(seed: int = 0, part: int = 0) -> dict:
    splits = jax.random.split(jax.random.key(seed), 5)
    own_keys = jax.random.split(jax.random.fold_in(splits[4], part), 5)
    signal = draw_signal(jax.random.fold_in(jax.random.fold_in(splits[4], part), 71), part)
    coverage = touch_ends((jax.random.randint(own_keys[1], (SAMPLES, POSITIONS), 0, 5) < 4).astype(jnp.int32), jax.random.fold_in(own_keys[1], 1), 0, 1)
    design_codes = touch_ends(jax.random.randint(splits[2], (CODES, SAMPLES), 0, 5), jax.random.fold_in(splits[2], 1), 0, 4).astype(jnp.int32)
    level_prior = jnp.clip(jnp.exp(jax.random.uniform(splits[3], (LEVELS + 1,), jnp.float32, math.log(0.1), math.log(10.0))), 0.1, 10.0)
    return dict(signal=signal, coverage=coverage, design_codes=design_codes, level_prior=level_prior)


LOWPASS = (0.23037781330885523, 0.7148465705525415, 0.6308807679295904, -0.02798376941698385, -0.18703481171888114, 0.030841381835986965, 0.032883011666982945, -0.010597401784997278)
HIGHPASS = tuple(((-1.0) ** number * LOWPASS[7 - number] for number in range(8)))
PRECISE = lax.Precision.HIGHEST

def analysis(signal_row):
    evens = signal_row[0::2]
    odds = signal_row[1::2]
    lower = jnp.zeros_like(evens)
    upper = jnp.zeros_like(evens)
    for shift_count in range(4):
        moved_even = jnp.roll(evens, -shift_count)
        moved_odd = jnp.roll(odds, -shift_count)
        lower = lower + LOWPASS[2 * shift_count] * moved_even + LOWPASS[2 * shift_count + 1] * moved_odd
        upper = upper + HIGHPASS[2 * shift_count] * moved_even + HIGHPASS[2 * shift_count + 1] * moved_odd
    return (lower, upper)

def forward(signal_row):
    approx = signal_row
    pieces = []
    for level_number in range(LEVELS):
        approx, detail = analysis(approx)
        pieces.append(detail)
    pieces.append(approx)
    return jnp.concatenate(pieces)

def synthesis(approx, detail):
    evens = jnp.zeros_like(approx)
    odds = jnp.zeros_like(approx)
    for shift_count in range(4):
        moved_approx = jnp.roll(approx, shift_count, axis=1)
        moved_detail = jnp.roll(detail, shift_count, axis=1)
        evens = evens + LOWPASS[2 * shift_count] * moved_approx + HIGHPASS[2 * shift_count] * moved_detail
        odds = odds + LOWPASS[2 * shift_count + 1] * moved_approx + HIGHPASS[2 * shift_count + 1] * moved_detail
    return jnp.stack([evens, odds], -1).reshape(approx.shape[0], 2 * approx.shape[1])

def reference(signal, coverage, design_codes, level_prior):

    def transform(row_pair):
        signal_row, mask_row = row_pair
        return forward(signal_row.astype(jnp.float32) * mask_row.astype(jnp.float32))
    coefficients = lax.map(transform, (signal, coverage))
    design = jnp.concatenate([jnp.ones((1, SAMPLES), jnp.float32), design_codes.astype(jnp.float32) - 2.0], 0)
    gram = jnp.dot(design, design.T, precision=PRECISE)
    moments = jnp.dot(design, coefficients, precision=PRECISE)
    factor = jnp.linalg.cholesky(gram)
    lower_inv = lax.linalg.triangular_solve(factor, jnp.eye(DESIGN, dtype=jnp.float32), left_side=True, lower=True)
    inverse_gram = jnp.dot(lower_inv.T, lower_inv, precision=PRECISE)
    effects = jnp.dot(inverse_gram, moments, precision=PRECISE)

    def accumulate(running, row_pair):
        column, coefficient_row = row_pair
        residual = coefficient_row - jnp.dot(column, effects, precision=PRECISE)
        return (running + residual * residual, None)
    squares, _unused = lax.scan(accumulate, jnp.zeros((POSITIONS,), jnp.float32), (design.T, coefficients))
    noise = squares / (SAMPLES - DESIGN) + 1e-06
    widths = [POSITIONS // 2 ** (number + 1) for number in range(LEVELS)] + [POSITIONS // 2 ** LEVELS]
    prior_columns = jnp.concatenate([jnp.broadcast_to(level_prior[number], (span_width,)) for number, span_width in enumerate(widths)])
    variance = noise[None, :] * jnp.diagonal(inverse_gram)[:, None] * prior_columns[None, :]
    squared = effects * effects
    shrunk = squared * effects / (squared + variance)
    current = shrunk[:, POSITIONS - widths[LEVELS]:]
    for number in reversed(range(LEVELS)):
        start = sum(widths[:number])
        current = synthesis(current, shrunk[:, start:start + widths[number]])
    return current
```

```python
import functools

import jax
import jax.numpy as jnp
import ml_dtypes
import numpy as np
from jax import lax
from jax.experimental import pallas as pl
from jax.experimental.pallas import tpu as pltpu
from jax.sharding import PartitionSpec as P

LEVELS = 10
DESIGN = 8
FINE = 4
BLOCK = 256
LOWPASS = np.array(
    (
        0.23037781330885523,
        0.7148465705525415,
        0.6308807679295904,
        -0.02798376941698385,
        -0.18703481171888114,
        0.030841381835986965,
        0.032883011666982945,
        -0.010597401784997278,
    )
)
HIGHPASS = np.array([(-1.0) ** m * LOWPASS[7 - m] for m in range(8)])


def spread(taps, step):
    out = np.zeros(7 * step + 1)
    out[::step] = taps
    return out


def composite(levels):
    low = np.ones(1)
    details = []
    for j in range(levels):
        details.append(np.convolve(low, spread(HIGHPASS, 2**j)))
        low = np.convolve(low, spread(LOWPASS, 2**j))
    return details, low


def column(taps, start, size):
    out = np.zeros(size)
    for i, tap in enumerate(taps):
        if 0 <= start + i < size:
            out[start + i] = tap
    return out


def tables(length):
    det, low = composite(LEVELS)
    fine_low = composite(FINE)[1]
    coarse_det, coarse_low = composite(LEVELS - FINE)
    cells = length >> FINE
    group1 = [(1, k) for k in range(125)] + [(2, k) for k in range(3)]
    group2 = [(0, k) for k in range(16)] + [(4, k) for k in range(16)] + [(3, k) for k in range(32)]
    group2 += [(2, k) for k in range(3, 64)] + [(1, k) for k in range(125, 128)]
    wide = np.zeros((BLOCK + 128, 2 * 128))
    level_main = np.zeros(256, np.int32)
    straddles = np.zeros(256, bool)
    for c, (level, k) in enumerate(group1 + group2):
        taps = det[level - 1] if level else fine_low
        step = 2 ** (level or FINE)
        wide[:, c] = column(taps, step * k, BLOCK + 128)
        level_main[c] = (level or 1) - 1
        straddles[c] = level > 0 and step * k + len(taps) > BLOCK
    coarse = [(level, k) for level in range(FINE + 1, LEVELS + 1) for k in range(length >> level)]
    coarse += [(0, k) for k in range(length >> LEVELS)]
    table_e = np.zeros((cells, 128))
    level_e = np.zeros(128, np.int32)
    for c, (level, k) in enumerate(coarse):
        taps = coarse_det[level - FINE - 1] if level else coarse_low
        step = 2 ** ((level or LEVELS) - FINE)
        level_e[c] = level - 1 if level else LEVELS
        full = det[level - 1] if level else low
        if (step << FINE) * k + len(full) <= length:
            table_e[:, c] = column(taps, step * k, cells)
    edge = []
    for level in range(1, LEVELS + 1):
        size = length >> level
        first = -(-(length - len(det[level - 1]) + 1) // 2**level)
        edge += [(level, k) for k in range(max(first, 0), size)]
    early = [e for e in edge if e[0] <= FINE]
    middle = [e for e in edge if FINE < e[0] < 9 or (e[0] == 9 and e[1] < 2)]
    late = [e for e in edge if e not in early + middle] + [(0, k) for k in range(length >> LEVELS)]
    rows = early + [None] * (24 - len(early)) + middle + [None] * (32 - len(middle))
    rows += late + [None] * (8 - len(late))
    level_u = np.zeros(128, np.int32)
    for r, row in enumerate(rows):
        if row:
            level_u[r] = row[0] - 1 if row[0] else LEVELS
    shifted = [(row, length) for row in rows] + [(row, 2 * length) for row in rows[56:]]
    shifted += [(row, 3 * length) for row in rows[56:]] + [(row, 0) for row in rows]
    edge_cells = np.zeros((144, cells))
    edge_first = np.zeros((80, 128))
    edge_last = np.zeros((64, BLOCK))
    halo = 6 * (2**FINE - 1)
    for r, (row, shift) in enumerate(shifted):
        if row is None:
            continue
        level, k = row
        if 1 <= level <= FINE:
            start = k * 2**level - shift
            if shift == 0:
                edge_last[r - 80] = column(det[level - 1], start - (length - BLOCK), BLOCK)
            elif shift == length:
                edge_first[r] = column(det[level - 1], start, 128)
            continue
        taps = coarse_det[level - FINE - 1] if level else coarse_low
        start = k * 2 ** ((level or LEVELS) - FINE) - (shift >> FINE)
        edge_cells[r] = column(taps, start, cells)
        for c in range(-6, 0):
            if 0 <= c - start < len(taps):
                edge_first[r] += taps[c - start] * column(fine_low, c * 2**FINE, 128)
    dense = np.stack([column(fine_low, k * 2**FINE, length) for k in range(cells)], 1)
    return dense, wide, table_e, edge_cells, edge_first, edge_last, level_main, level_e, level_u, straddles


def two(table):
    high = table.astype(np.float32).astype(ml_dtypes.bfloat16)
    rest = (table - high.astype(np.float64)).astype(np.float32).astype(ml_dtypes.bfloat16)
    return np.stack([high, rest])


NN = (((1,), (0,)), ((), ()))
NT = (((1,), (1,)), ((), ()))


def dot(a, b, dims):
    return lax.dot_general(a, b, dims, preferred_element_type=jnp.float32)


def halves(a):
    high = a.astype(jnp.bfloat16)
    return high, (a - high.astype(jnp.float32)).astype(jnp.bfloat16)


def dot3(a, b, dims):
    return dot(a[0], b[0], dims) + dot(a[0], b[1], dims) + dot(a[1], b[0], dims)


CHUNK = 512
F32 = jnp.float32
BF16 = jnp.bfloat16


def kernel(total, *refs):
    inputs = refs[:12]
    out = refs[12]
    loaded = refs[13:25]
    (
        d_ref,
        xe,
        sent,
        near,
        far2,
        far3,
        gram_mine,
        gram_theirs,
        stats_mine,
        stats_theirs,
        edge_mine,
        edge_theirs,
        su_ref,
        su_got,
        stack,
        y_ref,
        load_sem,
        send_sem,
        recv_sem,
    ) = refs[25:]
    signal, coverage = loaded[:2]
    codes, prior, levels, dead, dense, wide, table_e, edge_cells, edge_first, edge_last = loaded[2:]
    samples, length = signal.shape
    blocks = length // BLOCK
    chunks = length // CHUNK
    width = blocks * BLOCK + 128
    me = lax.axis_index("genome")
    peers = lax.axis_size("genome")
    side = lax.axis_index("sample")
    before = [lax.rem(me + peers - i, peers) for i in (1, 2, 3)]
    after = [lax.rem(me + i, peers) for i in (1, 2, 3)]

    barrier = pltpu.get_barrier_semaphore()
    for peer in before + after:
        pl.semaphore_signal(barrier, inc=1, device_id={"genome": peer})
    pl.semaphore_signal(barrier, inc=1, device_id={"sample": 1 - side})

    loads = {}

    def load(name, src, dst):
        c = pltpu.make_async_copy(src, dst, load_sem.at[len(loads)])
        c.start()
        loads[name] = c

    def load_chunk(i):
        span = pl.ds(i * CHUNK, CHUNK)
        load(("signal", i), inputs[0].at[:, span], signal.at[:, span])
        load(("coverage", i), inputs[1].at[:, span], coverage.at[:, span])

    names = ("codes", "prior", "levels", "dead", "dense", "wide", "table_e", "cells", "first", "last")
    later = dict(zip(names, zip(inputs[2:], loaded[2:])))
    load("codes", *later["codes"])
    load_chunk(0)
    load("first", *later["first"])
    load("dense", *later["dense"])
    for i in range(1, chunks):
        load_chunk(i)
    for name in ("cells", "last", "table_e", "wide", "prior", "levels", "dead"):
        load(name, *later[name])

    def copy(number, src, dst, device):
        return pltpu.make_async_remote_copy(
            src_ref=src,
            dst_ref=dst,
            send_sem=send_sem.at[number],
            recv_sem=recv_sem.at[number],
            device_id=device,
            device_id_type=pl.DeviceIdType.MESH,
        )

    loads["codes"].wait()
    d_ref[0:1, :] = jnp.ones((1, samples), F32)
    d_ref[1:8, :] = codes[...].astype(F32) - 2.0
    design = d_ref[...].astype(BF16)
    padded = jnp.concatenate([d_ref[...], jnp.zeros((120, samples), F32)], 0)
    gram_mine[...] = dot(design, padded.astype(BF16), NT)

    edge_copies = []
    a4 = None
    for i in range(chunks):
        loads["signal", i].wait()
        loads["coverage", i].wait()
        span = slice(i * CHUNK, (i + 1) * CHUNK)
        x = (signal[:, span].astype(F32) * coverage[:, span].astype(F32)).astype(BF16)
        xe[:samples, span] = x
        if i == 0:
            loads["first"].wait()
            first = dot(edge_first[0], x[:, :128], NT) + dot(edge_first[1], x[:, :128], NT)
            sent[0:24] = first[0:24]
            pl.semaphore_wait(barrier, 7)
            edge_copies.append(copy(1, sent.at[0:24], near.at[0:24], {"genome": before[0]}))
            edge_copies[0].start()
            gram_copy = copy(0, gram_mine, gram_theirs, {"sample": 1 - side})
            gram_copy.start()
            loads["dense"].wait()
        piece = dot(x, dense[span], NN)
        a4 = piece if a4 is None else a4 + piece
    a4 = halves(a4[:, :128] + a4[:, 128:])

    loads["cells"].wait()
    there = (edge_cells[0, 16:80], edge_cells[1, 16:80])
    sent[24:80] = dot3(there, a4, NT)[8:] + first[24:80]
    edge_copies += [
        copy(2, sent.at[64:72], far2, {"genome": before[1]}),
        copy(3, sent.at[72:80], far3, {"genome": before[2]}),
        copy(9, sent.at[24:64], near.at[24:64], {"genome": before[0]}),
    ]
    for c in edge_copies[1:]:
        c.start()

    for name in ("table_e", "wide", "last"):
        loads[name].wait()
    for b in range(blocks):
        span = slice(b * BLOCK, (b + 1) * BLOCK)
        p = dot(design, xe[:samples, span], NN)
        high = p.astype(BF16).astype(F32)
        xe[samples:, span] = jnp.concatenate([high, p - high], 0).astype(BF16)
    e = dot3(a4, (table_e[0], table_e[1]), NN)
    eh, el = halves(e)
    stats_mine[0:8, width - 128 : width] = dot(design, eh, NN) + dot(design, el, NN)
    stats_mine[8:16, width - 128 : width] = jnp.sum((e * e).reshape(samples // 8, 8, 128), 0)
    for b in range(blocks):
        depth = BLOCK + 128 if b < blocks - 1 else BLOCK
        span = slice(b * BLOCK, (b + 1) * BLOCK)
        rows = xe[:, b * BLOCK : b * BLOCK + depth]
        res = dot(rows, wide[0, :depth], NN) + dot(rows, wide[1, :depth], NN)
        main = res[:samples]
        stats_mine[0:8, span] = res[samples : samples + 8] + res[samples + 8 :]
        stats_mine[8:16, span] = jnp.sum((main * main).reshape(samples // 8, 8, BLOCK), 0)
    stats_copy = copy(4, stats_mine, stats_theirs, {"sample": 1 - side})
    stats_copy.start()
    end_cells = xe[:samples, length - BLOCK : length]
    own = dot3((edge_cells[0, 80:144], edge_cells[1, 80:144]), a4, NT) + dot(edge_last[0], end_cells, NT) + dot(edge_last[1], end_cells, NT)

    gram_copy.wait()
    for name in ("prior", "levels", "dead"):
        loads[name].wait()
    lanes = lax.broadcasted_iota(jnp.int32, (8, 128), 1)
    subs = lax.broadcasted_iota(jnp.int32, (8, 128), 0)
    aug = gram_mine[...] + gram_theirs[...] + jnp.where(lanes == subs + 8, 1.0, 0.0)
    for k in range(DESIGN):
        row = aug[k : k + 1, :] / aug[k : k + 1, k : k + 1]
        aug = jnp.where(subs == k, row, aug - aug[:, k : k + 1] * row)
    diagonal = jnp.sum(jnp.where(lanes == subs + 8, aug, 0.0), 1, keepdims=True)
    inverse = [aug[:, 8 + k : 9 + k] for k in range(DESIGN)]
    weights = jnp.zeros(levels.shape, F32)
    for number in range(LEVELS + 1):
        weights = jnp.where(levels[...] == number, prior[number], weights)

    def shrink(m, s, weight):
        effects = inverse[0] * m[0:1]
        for k in range(1, DESIGN):
            effects = effects + inverse[k] * m[k : k + 1]
        left = jnp.sum(s, 0, keepdims=True) - jnp.sum(m * effects, 0, keepdims=True)
        noise = jnp.maximum(left, 0.0) / (total - DESIGN) + 1e-06
        squared = effects * effects
        return squared * effects / (squared + (noise * weight) * diagonal)

    for c in edge_copies:
        c.wait()
    u = own + near[...]
    u = jnp.concatenate([u[:56], u[56:] + far2[...] + far3[...], jnp.zeros((64, samples), F32)], 0)
    uh, ul = halves(u)
    sh, sl = halves(u * u)
    only = jnp.where(lax.broadcasted_iota(jnp.int32, (8, samples), 0) == 0, 1.0, 0.0)
    only = only.astype(BF16)
    edge_mine[0:8] = dot(design, uh, NT) + dot(design, ul, NT)
    edge_mine[8:16] = dot(only, sh, NT) + dot(only, sl, NT)
    edge_copy = copy(5, edge_mine, edge_theirs, {"sample": 1 - side})
    edge_copy.start()

    stats_copy.wait()

    def paired(shrunk):
        high = shrunk.astype(BF16).astype(F32)
        return jnp.concatenate([high, shrunk - high], 0).astype(BF16)

    def both(a, table, dims):
        return dot(a, table[0], dims) + dot(a, table[1], dims)

    def folded(res):
        return res[:8] + res[8:]

    lane = lax.broadcasted_iota(jnp.int32, (8, BLOCK), 1)
    coarse = (lane >= 128) & (lane < 144)
    for b in range(blocks):
        span = slice(b * BLOCK, (b + 1) * BLOCK)
        m = stats_mine[0:8, span] + stats_theirs[0:8, span]
        s = stats_mine[8:16, span] + stats_theirs[8:16, span]
        g = jnp.where(coarse, 0.0, shrink(m, s, weights[:, :BLOCK]))
        if b == blocks - 1:
            g = jnp.where(dead[...] > 0, 0.0, g)
        stack[16 * b : 16 * b + 16, :] = paired(g)
    span = slice(width - 128, width)
    m = stats_mine[0:8, span] + stats_theirs[0:8, span]
    s = stats_mine[8:16, span] + stats_theirs[8:16, span]
    se = paired(shrink(m, s, weights[:, BLOCK : BLOCK + 128]))

    edge_copy.wait()
    m = edge_mine[0:8] + edge_theirs[0:8]
    s = edge_mine[8:16] + edge_theirs[8:16]
    su_ref[...] = shrink(m, s, weights[:, BLOCK + 128 :])
    su_copies = [copy(6 + i, su_ref, su_got.at[i], {"genome": after[i]}) for i in range(3)]
    for c in su_copies:
        c.start()

    y = both(stack[...], (wide[0], wide[1]), NT)
    su = paired(su_ref[...])[:, :64]
    a4 = both(se, (table_e[0], table_e[1]), NT) + both(
        su, (edge_cells[0, 80:144], edge_cells[1, 80:144]), NN
    )
    tail = folded(both(su, (edge_last[0], edge_last[1]), NN))
    for c in su_copies:
        c.wait()
    got = [paired(su_got[i]) for i in range(3)]
    begin = jnp.zeros((16, 128), F32)
    for piece, lo, hi in ((got[0][:, :64], 0, 64), (got[1][:, 56:64], 64, 72), (got[2][:, 56:64], 72, 80)):
        a4 = a4 + both(piece, (edge_cells[0, lo:hi], edge_cells[1, lo:hi]), NN)
        begin = begin + both(piece, (edge_first[0, lo:hi], edge_first[1, lo:hi]), NN)
    a4 = folded(a4)
    begin = folded(begin)
    narrow = lax.broadcasted_iota(jnp.int32, (8, 128), 1) < 16
    for b in range(blocks):
        moved = a4 if b == 0 else pltpu.roll(a4, 128 - 16 * b, 1)
        stack[16 * b : 16 * b + 16, :128] = paired(jnp.where(narrow, moved, 0.0))
    y = y + both(stack[:, :128], (wide[0, :, 128:256], wide[1, :, 128:256]), NT)
    for b in range(blocks):
        piece = folded(y[16 * b : 16 * b + 16])
        y_ref[:, b * BLOCK : b * BLOCK + 128] = piece[:, :128] + begin
        second = piece[:, 128:256]
        if b == blocks - 1:
            y_ref[:, b * BLOCK : b * BLOCK + 128] += tail[:, :128]
            second = second + tail[:, 128:]
        y_ref[:, b * BLOCK + 128 : (b + 1) * BLOCK] = second
        begin = piece[:, 256:]
    out[...] = jnp.where(side == 0, y_ref[0:4], y_ref[4:8])


def local(signal, coverage, design_codes, level_prior):
    samples, length = signal.shape
    blocks = length // BLOCK
    dense, *pairs, l_main, l_e, l_u, straddles = tables(length)
    dense = jnp.asarray(np.concatenate(list(two(dense)), 1))
    pieces = [jnp.asarray(two(t)) for t in pairs]
    levels = jnp.asarray(np.concatenate([l_main, l_e, l_u])[None])
    dead = jnp.asarray(straddles.astype(np.int32)[None])
    total = samples * lax.axis_size("sample")
    width = blocks * BLOCK + 128
    operands = (signal, coverage, design_codes, level_prior, levels, dead, dense, *pieces)
    places = [pltpu.VMEM(a.shape, a.dtype) for a in operands]
    places[3] = pltpu.SMEM(level_prior.shape, F32)
    copies = 10
    return pl.pallas_call(
        functools.partial(kernel, total),
        out_shape=pltpu.VMEM((DESIGN // lax.axis_size("sample"), length), F32),
        in_specs=[pl.BlockSpec(memory_space=pltpu.HBM)] * len(operands),
        out_specs=pl.BlockSpec(memory_space=pltpu.VMEM),
        scratch_shapes=places
        + [
            pltpu.VMEM((8, samples), F32),
            pltpu.VMEM((samples + 16, length), BF16),
            pltpu.VMEM((80, samples), F32),
            pltpu.VMEM((64, samples), F32),
            pltpu.VMEM((8, samples), F32),
            pltpu.VMEM((8, samples), F32),
            pltpu.VMEM((8, 128), F32),
            pltpu.VMEM((8, 128), F32),
            pltpu.VMEM((16, width), F32),
            pltpu.VMEM((16, width), F32),
            pltpu.VMEM((16, 128), F32),
            pltpu.VMEM((16, 128), F32),
            pltpu.VMEM((8, 128), F32),
            pltpu.VMEM((3, 8, 128), F32),
            pltpu.VMEM((16 * blocks, BLOCK), BF16),
            pltpu.VMEM((8, length), F32),
            pltpu.SemaphoreType.DMA((10 + 2 * (length // CHUNK),)),
            pltpu.SemaphoreType.DMA((copies,)),
            pltpu.SemaphoreType.DMA((copies,)),
        ],
        compiler_params=pltpu.CompilerParams(
            collective_id=0, has_side_effects=True, vmem_limit_bytes=56 * 2**20
        ),
    )(*operands)


def solution(mesh):
    placed = (
        P("sample", ("parts", "genome")),
        P("sample", ("parts", "genome")),
        P(None, "sample"),
        P(),
    )
    return jax.shard_map(
        local,
        mesh=mesh,
        in_specs=placed,
        out_specs=P("sample", ("parts", "genome")),
        check_vma=False,
    )
```

```python
import functools

import jax
import jax.numpy as jnp
import ml_dtypes
import numpy as np
from jax import lax
from jax.experimental import pallas as pl
from jax.experimental.pallas import tpu as pltpu
from jax.sharding import PartitionSpec as P

LEVELS = 10
DESIGN = 8
FINE = 4
BLOCK = 256
TAIL = 512
LOWPASS = np.array(
    (
        0.23037781330885523,
        0.7148465705525415,
        0.6308807679295904,
        -0.02798376941698385,
        -0.18703481171888114,
        0.030841381835986965,
        0.032883011666982945,
        -0.010597401784997278,
    )
)
HIGHPASS = np.array([(-1.0) ** m * LOWPASS[7 - m] for m in range(8)])


def spread(taps, step):
    out = np.zeros(7 * step + 1)
    out[::step] = taps
    return out


def composite(levels):
    low = np.ones(1)
    details = []
    for j in range(levels):
        details.append(np.convolve(low, spread(HIGHPASS, 2**j)))
        low = np.convolve(low, spread(LOWPASS, 2**j))
    return details, low


def column(taps, start, size):
    out = np.zeros(size)
    for i, tap in enumerate(taps):
        if 0 <= start + i < size:
            out[start + i] = tap
    return out


def tables(length):
    det, low = composite(LEVELS)
    fine_low = composite(FINE)[1]
    coarse_det, coarse_low = composite(LEVELS - FINE)
    cells = length >> FINE
    group1 = [(1, k) for k in range(125)] + [(2, k) for k in range(3)]
    group2 = [(0, k) for k in range(16)] + [(4, k) for k in range(16)] + [(3, k) for k in range(32)]
    group2 += [(2, k) for k in range(3, 64)] + [(1, k) for k in range(125, 128)]
    wide = np.zeros((BLOCK + 128, 2 * 128))
    level_main = np.zeros(256, np.int32)
    straddles = np.zeros(256, bool)
    for c, (level, k) in enumerate(group1 + group2):
        taps = det[level - 1] if level else fine_low
        step = 2 ** (level or FINE)
        wide[:, c] = column(taps, step * k, BLOCK + 128)
        level_main[c] = (level or 1) - 1
        straddles[c] = level > 0 and step * k + len(taps) > BLOCK
    coarse = [(level, k) for level in range(FINE + 1, LEVELS + 1) for k in range(length >> level)]
    coarse += [(0, k) for k in range(length >> LEVELS)]
    table_e = np.zeros((cells, 128))
    level_e = np.zeros(128, np.int32)
    for c, (level, k) in enumerate(coarse):
        taps = coarse_det[level - FINE - 1] if level else coarse_low
        step = 2 ** ((level or LEVELS) - FINE)
        level_e[c] = level - 1 if level else LEVELS
        full = det[level - 1] if level else low
        if (step << FINE) * k + len(full) <= length:
            table_e[:, c] = column(taps, step * k, cells)
    edge = []
    for level in range(1, LEVELS + 1):
        size = length >> level
        first = -(-(length - len(det[level - 1]) + 1) // 2**level)
        edge += [(level, k) for k in range(max(first, 0), size)]
    early = [e for e in edge if e[0] < 7]
    middle = [e for e in edge if 7 <= e[0] < 9 or (e[0] == 9 and e[1] < 2)]
    late = [e for e in edge if e not in early + middle] + [(0, k) for k in range(length >> LEVELS)]
    early += [None] * (32 - len(early))
    middle += [None] * (16 - len(middle))
    late += [None] * (8 - len(late))
    level_p = np.zeros(128, np.int32)
    level_o = np.zeros(128, np.int32)
    for levels, rows in ((level_p, early + middle + 3 * late), (level_o, early + middle + late)):
        for r, row in enumerate(rows):
            if row:
                levels[r] = row[0] - 1 if row[0] else LEVELS
    shifted = [(row, 0) for row in middle + late] + [(row, length) for row in late]
    shifted += [(row, 2 * length) for row in late] + [(row, 3 * length) for row in late]
    shifted += [(row, length) for row in early + middle]
    edge_cells = np.zeros((96, cells))
    edge_first = np.zeros((96, 128))
    edge_last = np.zeros((32, TAIL))
    direct = np.zeros((80, length))
    for r, (row, shift) in enumerate(shifted):
        if row is None:
            continue
        level, k = row
        if shift:
            full = det[level - 1] if level else low
            direct[r - 48 if r >= 48 else r + 24] = column(full, k * 2 ** (level or LEVELS) - shift, length)
        if 1 <= level <= FINE:
            edge_first[r] = column(det[level - 1], k * 2**level - shift, 128)
            continue
        taps = coarse_det[level - FINE - 1] if level else coarse_low
        start = k * 2 ** ((level or LEVELS) - FINE) - (shift >> FINE)
        edge_cells[r] = column(taps, start, cells)
        for c in range(-6, 0):
            if 0 <= c - start < len(taps):
                edge_first[r] += taps[c - start] * column(fine_low, c * 2**FINE, 128)
    for r, row in enumerate(early):
        if row:
            edge_last[r] = column(det[row[0] - 1], row[1] * 2 ** row[0] - (length - TAIL), TAIL)
    base = np.stack([column(fine_low, (k if k < 16 else k - 128) * 2**FINE, BLOCK) for k in range(128)], 1)
    return base, wide, table_e, edge_cells, edge_first, edge_last, direct, level_main, level_e, level_p, level_o, straddles


def two(table):
    high = table.astype(np.float32).astype(ml_dtypes.bfloat16)
    rest = (table - high.astype(np.float64)).astype(np.float32).astype(ml_dtypes.bfloat16)
    return np.stack([high, rest])


NN = (((1,), (0,)), ((), ()))
NT = (((1,), (1,)), ((), ()))


def dot(a, b, dims):
    return lax.dot_general(a, b, dims, preferred_element_type=jnp.float32)


def halves(a):
    high = a.astype(jnp.bfloat16)
    return high, (a - high.astype(jnp.float32)).astype(jnp.bfloat16)


def dot3(a, b, dims):
    return dot(a[0], b[0], dims) + dot(a[0], b[1], dims) + dot(a[1], b[0], dims)


CHUNK = 512
F32 = jnp.float32
BF16 = jnp.bfloat16


def kernel(total, *refs):
    inputs = refs[:13]
    out = refs[13]
    loaded = refs[14:27]
    (
        d_ref,
        xe,
        dense,
        own_e,
        rows,
        got_e,
        got_m,
        got_2,
        got_3,
        back_1,
        back_2,
        back_3,
        gram_mine,
        gram_theirs,
        stats_mine,
        stats_theirs,
        own_mine,
        own_theirs,
        prev_mine,
        prev_theirs,
        stack,
        y_ref,
        load_sem,
        send_sem,
        recv_sem,
        present,
    ) = refs[27:]
    signal, coverage = loaded[:2]
    codes, prior, levels, dead, base, wide, table_e, edge_cells, edge_first, edge_last, direct = loaded[2:]
    samples, length = signal.shape
    blocks = length // BLOCK
    chunks = length // CHUNK
    width = blocks * BLOCK + 128
    me = lax.axis_index("genome")
    peers = lax.axis_size("genome")
    side = lax.axis_index("sample")
    before = [lax.rem(me + peers - i, peers) for i in (1, 2, 3)]
    after = [lax.rem(me + i, peers) for i in (1, 2, 3)]

    barrier = pltpu.get_barrier_semaphore()
    for peer in before:
        pl.semaphore_signal(barrier, inc=1, device_id={"genome": peer})
    pl.semaphore_signal(barrier, inc=1, device_id={"sample": 1 - side})

    loads = {}

    def load(name, src, dst):
        c = pltpu.make_async_copy(src, dst, load_sem.at[len(loads)])
        c.start()
        loads[name] = c

    def load_chunk(i):
        span = pl.ds(i * CHUNK, CHUNK)
        load(("signal", i), inputs[0].at[:, span], signal.at[:, span])
        load(("coverage", i), inputs[1].at[:, span], coverage.at[:, span])

    names = ("codes", "prior", "levels", "dead", "base", "wide", "table_e", "cells", "first", "last", "direct")
    later = dict(zip(names, zip(inputs[2:], loaded[2:])))
    order = [chunks - 1, *range(chunks - 1)]
    load("base", *later["base"])
    load("codes", *later["codes"])
    load_chunk(order[0])
    load("last", *later["last"])
    load_chunk(order[1])
    load("first", *later["first"])
    for i in order[2:]:
        load_chunk(i)
    load("cells", *later["cells"])

    def copy(number, src, dst, device):
        return pltpu.make_async_remote_copy(
            src_ref=src,
            dst_ref=dst,
            send_sem=send_sem.at[number],
            recv_sem=recv_sem.at[number],
            device_id=device,
            device_id_type=pl.DeviceIdType.MESH,
        )

    loads["codes"].wait()
    d_ref[0:1, :] = jnp.ones((1, samples), F32)
    d_ref[1:8, :] = codes[...].astype(F32) - 2.0
    design = d_ref[...].astype(BF16)
    padded = jnp.concatenate([d_ref[...], jnp.zeros((120, samples), F32)], 0)
    gram_mine[...] = dot(design, padded.astype(BF16), NT)
    loads["base"].wait()
    for half in range(2):
        part = base[half].astype(F32)
        lane = lax.broadcasted_iota(jnp.int32, part.shape, 1)
        for b in range(blocks):
            moved = jnp.where(lane < 16, part, 0.0) if b == 0 else pltpu.roll(part, 16 * b, 1)
            dense[b * BLOCK : (b + 1) * BLOCK, half * 128 : half * 128 + 128] = moved.astype(BF16)

    a4 = None
    for i in order:
        loads["signal", i].wait()
        loads["coverage", i].wait()
        span = slice(i * CHUNK, (i + 1) * CHUNK)
        x = (signal[:, span].astype(F32) * coverage[:, span].astype(F32)).astype(BF16)
        xe[:samples, span] = x
        if i == chunks - 1:
            loads["last"].wait()
            own_e[...] = dot(edge_last[0], x, NT) + dot(edge_last[1], x, NT)
            pl.semaphore_wait(barrier, 4)
            forward = [copy(0, own_e, got_e, {"genome": after[0]})]
            forward[0].start()
            gram_copy = copy(1, gram_mine, gram_theirs, {"sample": 1 - side})
            gram_copy.start()
            for peer in after:
                pl.semaphore_signal(present, inc=1, device_id={"genome": peer})
        if i == 0:
            loads["first"].wait()
            first = dot(edge_first[0], x[:, :128], NT) + dot(edge_first[1], x[:, :128], NT)
        piece = dot(x, dense[span], NN)
        a4 = piece if a4 is None else a4 + piece
    a4 = halves(a4[:, :128] + a4[:, 128:])

    loads["cells"].wait()
    rows[0:48] = dot3((edge_cells[0, 0:48], edge_cells[1, 0:48]), a4, NT) + first[0:48]
    forward += [
        copy(2, rows.at[0:40], got_m, {"genome": after[0]}),
        copy(3, rows.at[16:32], got_2, {"genome": after[1]}),
        copy(4, rows.at[16:24], got_3, {"genome": after[2]}),
    ]
    for c in forward[1:]:
        c.start()
    for name in ("table_e", "wide", "prior", "levels", "dead", "direct"):
        load(name, *later[name])
    rows[48:96] = dot3((edge_cells[0, 48:96], edge_cells[1, 48:96]), a4, NT) + first[48:96]

    for b in range(blocks):
        span = slice(b * BLOCK, (b + 1) * BLOCK)
        p = dot(design, xe[:samples, span], NN)
        high = p.astype(BF16).astype(F32)
        xe[samples:, span] = jnp.concatenate([high, p - high], 0).astype(BF16)
    for name in ("table_e", "wide"):
        loads[name].wait()
    e = dot3(a4, (table_e[0], table_e[1]), NN)
    eh, el = halves(e)
    stats_mine[0:8, width - 128 : width] = dot(design, eh, NN) + dot(design, el, NN)
    stats_mine[8:16, width - 128 : width] = jnp.sum((e * e).reshape(samples // 8, 8, 128), 0)
    for b in range(blocks):
        depth = BLOCK + 128 if b < blocks - 1 else BLOCK
        span = slice(b * BLOCK, (b + 1) * BLOCK)
        window = xe[:, b * BLOCK : b * BLOCK + depth]
        res = dot(window, wide[0, :depth], NN) + dot(window, wide[1, :depth], NN)
        main = res[:samples]
        stats_mine[0:8, span] = res[samples : samples + 8] + res[samples + 8 :]
        stats_mine[8:16, span] = jnp.sum((main * main).reshape(samples // 8, 8, BLOCK), 0)
    stats_copy = copy(5, stats_mine, stats_theirs, {"sample": 1 - side})
    stats_copy.start()

    pl.semaphore_wait(present, 3)
    backward = [
        copy(6, rows.at[24:96], back_1, {"genome": before[0]}),
        copy(7, rows.at[32:48], back_2, {"genome": before[1]}),
        copy(8, rows.at[40:48], back_3, {"genome": before[2]}),
    ]
    for c in backward:
        c.start()

    gram_copy.wait()
    for name in ("prior", "levels", "dead", "direct"):
        loads[name].wait()
    lanes = lax.broadcasted_iota(jnp.int32, (8, 128), 1)
    subs = lax.broadcasted_iota(jnp.int32, (8, 128), 0)
    aug = gram_mine[...] + gram_theirs[...] + jnp.where(lanes == subs + 8, 1.0, 0.0)
    for k in range(DESIGN):
        row = aug[k : k + 1, :] / aug[k : k + 1, k : k + 1]
        aug = jnp.where(subs == k, row, aug - aug[:, k : k + 1] * row)
    diagonal = jnp.sum(jnp.where(lanes == subs + 8, aug, 0.0), 1, keepdims=True)
    inverse = [aug[:, 8 + k : 9 + k] for k in range(DESIGN)]
    weights = jnp.zeros(levels.shape, F32)
    for number in range(LEVELS + 1):
        weights = jnp.where(levels[...] == number, prior[number], weights)

    def shrink(m, s, weight):
        effects = inverse[0] * m[0:1]
        for k in range(1, DESIGN):
            effects = effects + inverse[k] * m[k : k + 1]
        left = jnp.sum(s, 0, keepdims=True) - jnp.sum(m * effects, 0, keepdims=True)
        noise = jnp.maximum(left, 0.0) / (total - DESIGN) + 1e-06
        squared = effects * effects
        return squared * effects / (squared + (noise * weight) * diagonal)

    def paired(shrunk):
        high = shrunk.astype(BF16).astype(F32)
        return jnp.concatenate([high, shrunk - high], 0).astype(BF16)

    def both(a, table, dims):
        return dot(a, table[0], dims) + dot(a, table[1], dims)

    def folded(res):
        return res[:8] + res[8:]

    def pick(a):
        return jnp.where(side == 0, a[:4], a[4:])

    stats_copy.wait()
    lane = lax.broadcasted_iota(jnp.int32, (8, BLOCK), 1)
    coarse = (lane >= 128) & (lane < 144)
    for b in range(blocks):
        span = slice(b * BLOCK, (b + 1) * BLOCK)
        m = stats_mine[0:8, span] + stats_theirs[0:8, span]
        s = stats_mine[8:16, span] + stats_theirs[8:16, span]
        g = jnp.where(coarse, 0.0, shrink(m, s, weights[:, :BLOCK]))
        if b == blocks - 1:
            g = jnp.where(dead[...] > 0, 0.0, g)
        stack[16 * b : 16 * b + 16, :] = paired(g)
    span = slice(width - 128, width)
    m = stats_mine[0:8, span] + stats_theirs[0:8, span]
    s = stats_mine[8:16, span] + stats_theirs[8:16, span]
    se = paired(shrink(m, s, weights[:, BLOCK : BLOCK + 128]))
    y = both(stack[...], (wide[0], wide[1]), NT)
    a4 = both(se, (table_e[0], table_e[1]), NT)

    only = jnp.where(lax.broadcasted_iota(jnp.int32, (8, samples), 0) == 0, 1.0, 0.0)
    only = only.astype(BF16)

    def summed(u, ref):
        u = jnp.concatenate([u, jnp.zeros((128 - u.shape[0], samples), F32)], 0)
        uh, ul = halves(u)
        sh, sl = halves(u * u)
        ref[0:8] = dot(design, uh, NT) + dot(design, ul, NT)
        ref[8:16] = dot(only, sh, NT) + dot(only, sl, NT)

    for c in backward:
        c.wait()
    u = jnp.concatenate(
        [
            own_e[...] + back_1[24:56],
            rows[0:16] + back_1[56:72],
            rows[16:24] + back_1[0:8] + back_2[0:8] + back_3[...],
        ],
        0,
    )
    summed(u, own_mine)
    own_copy = copy(9, own_mine, own_theirs, {"sample": 1 - side})
    own_copy.start()

    for c in forward:
        c.wait()
    u = jnp.concatenate(
        [
            rows[48:80] + got_e[...],
            rows[80:96] + got_m[0:16],
            rows[24:32] + got_m[16:24] + back_1[8:16] + back_2[8:16],
            rows[32:40] + got_m[24:32] + got_2[0:8] + back_1[16:24],
            rows[40:48] + got_m[32:40] + got_2[8:16] + got_3[...],
        ],
        0,
    )
    summed(u, prev_mine)
    prev_copy = copy(10, prev_mine, prev_theirs, {"sample": 1 - side})
    prev_copy.start()

    own_copy.wait()
    m = own_mine[0:8] + own_theirs[0:8]
    s = own_mine[8:16] + own_theirs[8:16]
    su = paired(shrink(m, s, weights[:, BLOCK + 256 :]))
    a4 = folded(a4 + both(su[:, 32:64], (edge_cells[0, :32], edge_cells[1, :32]), NN))
    tail = folded(both(su[:, :32], (edge_last[0], edge_last[1]), NN))
    narrow = lax.broadcasted_iota(jnp.int32, (8, 128), 1) < 16
    for b in range(blocks):
        moved = a4 if b == 0 else pltpu.roll(a4, 128 - 16 * b, 1)
        stack[16 * b : 16 * b + 16, :128] = paired(jnp.where(narrow, moved, 0.0))
    y = y + both(stack[:, :128], (wide[0, :, 128:256], wide[1, :, 128:256]), NT)
    begin = jnp.zeros((8, 128), F32)
    for b in range(blocks):
        piece = folded(y[16 * b : 16 * b + 16])
        parts = [piece[:, :128] + begin, piece[:, 128:256]]
        for h in range(2):
            at = b * BLOCK + h * 128
            if at >= length - TAIL:
                parts[h] = parts[h] + tail[:, at - length + TAIL : at - length + TAIL + 128]
            y_ref[:, at : at + 128] = pick(parts[h])
        begin = piece[:, 256:]

    prev_copy.wait()
    m = prev_mine[0:8] + prev_theirs[0:8]
    s = prev_mine[8:16] + prev_theirs[8:16]
    su = pick(shrink(m, s, weights[:, BLOCK + 128 : BLOCK + 256]))
    last = both(paired(su)[:, :80], (direct[0], direct[1]), NN)
    out[...] = y_ref[...] + last[:4] + last[4:]


def local(signal, coverage, design_codes, level_prior):
    samples, length = signal.shape
    blocks = length // BLOCK
    *pairs, l_main, l_e, l_p, l_o, straddles = tables(length)
    pieces = [jnp.asarray(two(t)) for t in pairs]
    levels = jnp.asarray(np.concatenate([l_main, l_e, l_p, l_o])[None])
    dead = jnp.asarray(straddles.astype(np.int32)[None])
    total = samples * lax.axis_size("sample")
    width = blocks * BLOCK + 128
    operands = (signal, coverage, design_codes, level_prior, levels, dead, *pieces)
    places = [pltpu.VMEM(a.shape, a.dtype) for a in operands]
    places[3] = pltpu.SMEM(level_prior.shape, F32)
    copies = 11
    return pl.pallas_call(
        functools.partial(kernel, total),
        out_shape=pltpu.VMEM((DESIGN // lax.axis_size("sample"), length), F32),
        in_specs=[pl.BlockSpec(memory_space=pltpu.HBM)] * len(operands),
        out_specs=pl.BlockSpec(memory_space=pltpu.VMEM),
        scratch_shapes=places
        + [
            pltpu.VMEM((8, samples), F32),
            pltpu.VMEM((samples + 16, length), BF16),
            pltpu.VMEM((length, 256), BF16),
            pltpu.VMEM((32, samples), F32),
            pltpu.VMEM((96, samples), F32),
            pltpu.VMEM((32, samples), F32),
            pltpu.VMEM((40, samples), F32),
            pltpu.VMEM((16, samples), F32),
            pltpu.VMEM((8, samples), F32),
            pltpu.VMEM((72, samples), F32),
            pltpu.VMEM((16, samples), F32),
            pltpu.VMEM((8, samples), F32),
            pltpu.VMEM((8, 128), F32),
            pltpu.VMEM((8, 128), F32),
            pltpu.VMEM((16, width), F32),
            pltpu.VMEM((16, width), F32),
            pltpu.VMEM((16, 128), F32),
            pltpu.VMEM((16, 128), F32),
            pltpu.VMEM((16, 128), F32),
            pltpu.VMEM((16, 128), F32),
            pltpu.VMEM((16 * blocks, BLOCK), BF16),
            pltpu.VMEM((4, length), F32),
            pltpu.SemaphoreType.DMA((11 + 2 * (length // CHUNK),)),
            pltpu.SemaphoreType.DMA((copies,)),
            pltpu.SemaphoreType.DMA((copies,)),
            pltpu.SemaphoreType.REGULAR,
        ],
        compiler_params=pltpu.CompilerParams(
            collective_id=0, has_side_effects=True, vmem_limit_bytes=56 * 2**20
        ),
    )(*operands)


def solution(mesh):
    placed = (
        P("sample", ("parts", "genome")),
        P("sample", ("parts", "genome")),
        P(None, "sample"),
        P(),
    )
    return jax.shard_map(
        local,
        mesh=mesh,
        in_specs=placed,
        out_specs=P("sample", ("parts", "genome")),
        check_vma=False,
    )
```

```python
import functools

import jax
import jax.numpy as jnp
import ml_dtypes
import numpy as np
from jax import lax
from jax.experimental import pallas as pl
from jax.experimental.pallas import tpu as pltpu
from jax.sharding import PartitionSpec as P

LEVELS = 10
DESIGN = 8
FINE = 4
BLOCK = 256
TAIL = 512
LOWPASS = np.array(
    (
        0.23037781330885523,
        0.7148465705525415,
        0.6308807679295904,
        -0.02798376941698385,
        -0.18703481171888114,
        0.030841381835986965,
        0.032883011666982945,
        -0.010597401784997278,
    )
)
HIGHPASS = np.array([(-1.0) ** m * LOWPASS[7 - m] for m in range(8)])


def spread(taps, step):
    out = np.zeros(7 * step + 1)
    out[::step] = taps
    return out


def composite(levels):
    low = np.ones(1)
    details = []
    for j in range(levels):
        details.append(np.convolve(low, spread(HIGHPASS, 2**j)))
        low = np.convolve(low, spread(LOWPASS, 2**j))
    return details, low


def column(taps, start, size):
    out = np.zeros(size)
    for i, tap in enumerate(taps):
        if 0 <= start + i < size:
            out[start + i] = tap
    return out


def tables(length):
    det, low = composite(LEVELS)
    fine_low = composite(FINE)[1]
    coarse_det, coarse_low = composite(LEVELS - FINE)
    cells = length >> FINE
    group1 = [(1, k) for k in range(125)] + [(2, k) for k in range(3)]
    group2 = [(0, k) for k in range(16)] + [(4, k) for k in range(16)] + [(3, k) for k in range(32)]
    group2 += [(2, k) for k in range(3, 64)] + [(1, k) for k in range(125, 128)]
    wide = np.zeros((BLOCK + 128, 2 * 128))
    level_main = np.zeros(256, np.int32)
    straddles = np.zeros(256, bool)
    for c, (level, k) in enumerate(group1 + group2):
        taps = det[level - 1] if level else fine_low
        step = 2 ** (level or FINE)
        wide[:, c] = column(taps, step * k, BLOCK + 128)
        level_main[c] = (level or 1) - 1
        straddles[c] = level > 0 and step * k + len(taps) > BLOCK
    coarse = [(level, k) for level in range(FINE + 1, LEVELS + 1) for k in range(length >> level)]
    coarse += [(0, k) for k in range(length >> LEVELS)]
    table_e = np.zeros((cells, 128))
    level_e = np.zeros(128, np.int32)
    for c, (level, k) in enumerate(coarse):
        taps = coarse_det[level - FINE - 1] if level else coarse_low
        step = 2 ** ((level or LEVELS) - FINE)
        level_e[c] = level - 1 if level else LEVELS
        full = det[level - 1] if level else low
        if (step << FINE) * k + len(full) <= length:
            table_e[:, c] = column(taps, step * k, cells)
    edge = []
    for level in range(1, LEVELS + 1):
        size = length >> level
        first = -(-(length - len(det[level - 1]) + 1) // 2**level)
        edge += [(level, k) for k in range(max(first, 0), size)]
    early = [e for e in edge if e[0] < 7]
    middle = [e for e in edge if 7 <= e[0] < 9 or (e[0] == 9 and e[1] < 2)]
    late = [e for e in edge if e not in early + middle] + [(0, k) for k in range(length >> LEVELS)]
    early += [None] * (32 - len(early))
    middle += [None] * (16 - len(middle))
    late += [None] * (8 - len(late))
    coarsest = late[2:6]
    none = [None] * 2
    sets = [row for row in late if row]
    levels = np.zeros(128, np.int32)
    for r, row in enumerate(early + middle + sets + sets + coarsest + late):
        if row:
            levels[r] = row[0] - 1 if row[0] else LEVELS
    shifted = []
    for shift, part in (
        (0, middle + sets), (1, sets), (2, coarsest),
        (0, 3 * none + sets), (1, coarsest),
        (0, 2 * none + coarsest),
        (1, sets), (2, sets), (3, coarsest),
        (2, sets), (3, sets), (0, 2 * none), (1, late),
        (3, late), (2, late),
        (0, late),
        (1, early + middle),
    ):
        shifted += [(row, shift * length) for row in part]
    edge_cells = np.zeros((176, cells))
    edge_first = np.zeros((176, 128))
    edge_last = np.zeros((32, TAIL))
    direct = np.zeros((80, length))
    into = {**{120 + r: r for r in range(48)}, **{56 + r: 48 + r for r in range(16)}, **{112 + r: 64 + r for r in range(8)}}
    for r, (row, shift) in enumerate(shifted):
        if row is None:
            continue
        level, k = row
        if r in into:
            full = det[level - 1] if level else low
            direct[into[r]] = column(full, k * 2 ** (level or LEVELS) - shift, length)
        if 1 <= level <= FINE:
            edge_first[r] = column(det[level - 1], k * 2**level - shift, 128)
            continue
        taps = coarse_det[level - FINE - 1] if level else coarse_low
        start = k * 2 ** ((level or LEVELS) - FINE) - (shift >> FINE)
        edge_cells[r] = column(taps, start, cells)
        for c in range(-6, 0):
            if 0 <= c - start < len(taps):
                edge_first[r] += taps[c - start] * column(fine_low, c * 2**FINE, 128)
    for r, row in enumerate(early):
        if row:
            edge_last[r] = column(det[row[0] - 1], row[1] * 2 ** row[0] - (length - TAIL), TAIL)
    base = np.stack([column(fine_low, (k if k < 16 else k - 128) * 2**FINE, BLOCK) for k in range(128)], 1)
    return base, wide, table_e, edge_cells, edge_first, edge_last, direct, level_main, level_e, levels, straddles


def two(table):
    high = table.astype(np.float32).astype(ml_dtypes.bfloat16)
    rest = (table - high.astype(np.float64)).astype(np.float32).astype(ml_dtypes.bfloat16)
    return np.stack([high, rest])


NN = (((1,), (0,)), ((), ()))
NT = (((1,), (1,)), ((), ()))


def dot(a, b, dims):
    return lax.dot_general(a, b, dims, preferred_element_type=jnp.float32)


def halves(a):
    high = a.astype(jnp.bfloat16)
    return high, (a - high.astype(jnp.float32)).astype(jnp.bfloat16)


def dot3(a, b, dims):
    return dot(a[0], b[0], dims) + dot(a[0], b[1], dims) + dot(a[1], b[0], dims)


CHUNK = 512
F32 = jnp.float32
BF16 = jnp.bfloat16


def kernel(total, *refs):
    inputs = refs[:13]
    out = refs[13]
    loaded = refs[14:27]
    (
        d_ref,
        xe,
        dense,
        own_e,
        rows,
        got_e,
        got_m,
        got_2,
        got_3,
        back_1,
        back_2,
        back_3,
        gram_mine,
        gram_theirs,
        stats_mine,
        stats_theirs,
        near,
        a_mine,
        a_theirs,
        b_mine,
        b_theirs,
        w_mine,
        w_theirs,
        su_ref,
        su_got,
        stack,
        y_ref,
        y_main,
        a4_main,
        load_sem,
        send_sem,
        recv_sem,
        present,
    ) = refs[27:]
    signal, coverage = loaded[:2]
    codes, prior, levels, dead, base, wide, table_e, edge_cells, edge_first, edge_last, direct = loaded[2:]
    samples, length = signal.shape
    blocks = length // BLOCK
    chunks = length // CHUNK
    width = blocks * BLOCK + 128
    me = lax.axis_index("genome")
    peers = lax.axis_size("genome")
    side = lax.axis_index("sample")
    before = [lax.rem(me + peers - i, peers) for i in (1, 2, 3)]
    after = [lax.rem(me + i, peers) for i in (1, 2, 3)]

    barrier = pltpu.get_barrier_semaphore()
    for peer in before:
        pl.semaphore_signal(barrier, inc=1, device_id={"genome": peer})
    pl.semaphore_signal(barrier, inc=1, device_id={"sample": 1 - side})

    loads = {}

    def load(name, src, dst):
        c = pltpu.make_async_copy(src, dst, load_sem.at[len(loads)])
        c.start()
        loads[name] = c

    def load_chunk(i):
        span = pl.ds(i * CHUNK, CHUNK)
        load(("signal", i), inputs[0].at[:, span], signal.at[:, span])
        load(("coverage", i), inputs[1].at[:, span], coverage.at[:, span])

    names = ("codes", "prior", "levels", "dead", "base", "wide", "table_e", "cells", "first", "last", "direct")
    later = dict(zip(names, zip(inputs[2:], loaded[2:])))
    order = [chunks - 1, *range(chunks - 1)]
    load("base", *later["base"])
    load("codes", *later["codes"])
    load_chunk(order[0])
    load("last", *later["last"])
    load_chunk(order[1])
    load("first", *later["first"])
    for i in order[2:]:
        load_chunk(i)
    load("cells", *later["cells"])

    def copy(number, src, dst, device):
        return pltpu.make_async_remote_copy(
            src_ref=src,
            dst_ref=dst,
            send_sem=send_sem.at[number],
            recv_sem=recv_sem.at[number],
            device_id=device,
            device_id_type=pl.DeviceIdType.MESH,
        )

    loads["codes"].wait()
    d_ref[0:1, :] = jnp.ones((1, samples), F32)
    d_ref[1:8, :] = codes[...].astype(F32) - 2.0
    design = d_ref[...].astype(BF16)
    padded = jnp.concatenate([d_ref[...], jnp.zeros((120, samples), F32)], 0)
    gram_mine[...] = dot(design, padded.astype(BF16), NT)
    loads["base"].wait()
    for half in range(2):
        part = base[half].astype(F32)
        lane = lax.broadcasted_iota(jnp.int32, part.shape, 1)
        for b in range(blocks):
            moved = jnp.where(lane < 16, part, 0.0) if b == 0 else pltpu.roll(part, 16 * b, 1)
            dense[b * BLOCK : (b + 1) * BLOCK, half * 128 : half * 128 + 128] = moved.astype(BF16)

    def enter():
        pl.semaphore_wait(barrier, 4)
        for i, peer in enumerate(after):
            pl.semaphore_signal(present.at[i], inc=1, device_id={"genome": peer})

    def send_last():
        forward[0].start()
        gram_copy.start()

    forward = [copy(0, own_e, got_e, {"genome": after[0]})]
    gram_copy = copy(1, gram_mine, gram_theirs, {"sample": 1 - side})
    pl.when(me >= peers // 2)(enter)
    a4 = None
    for i in order:
        loads["signal", i].wait()
        loads["coverage", i].wait()
        span = slice(i * CHUNK, (i + 1) * CHUNK)
        x = (signal[:, span].astype(F32) * coverage[:, span].astype(F32)).astype(BF16)
        xe[:samples, span] = x
        if i == chunks - 1:
            loads["last"].wait()
            own_e[...] = dot(edge_last[0], x, NT) + dot(edge_last[1], x, NT)
            pl.when(me >= peers // 2)(send_last)
        if i == 0:
            loads["first"].wait()
            first = dot(edge_first[0], x[:, :128], NT) + dot(edge_first[1], x[:, :128], NT)
        piece = dot(x, dense[span], NN)
        a4 = piece if a4 is None else a4 + piece
    a4 = halves(a4[:, :128] + a4[:, 128:])

    @pl.when(me < peers // 2)
    def _():
        enter()
        send_last()


    loads["cells"].wait()
    rows[0:64] = dot3((edge_cells[0, 0:64], edge_cells[1, 0:64]), a4, NT) + first[0:64]
    forward += [
        copy(2, rows.at[0:32], got_m, {"genome": after[0]}),
        copy(3, rows.at[32:48], got_2, {"genome": after[1]}),
        copy(4, rows.at[48:56], got_3, {"genome": after[2]}),
    ]
    for c in forward[1:]:
        c.start()
    for name in ("table_e", "wide", "prior", "levels", "dead", "direct"):
        load(name, *later[name])
    rows[64:176] = dot3((edge_cells[0, 64:176], edge_cells[1, 64:176]), a4, NT) + first[64:176]
    backward = [
        copy(6, rows.at[72:96], back_1, {"genome": before[0]}),
        copy(7, rows.at[96:112], back_2, {"genome": before[1]}),
        copy(8, rows.at[96:104], back_3, {"genome": before[2]}),
    ]
    near_copy = copy(12, rows.at[120:168], near, {"genome": before[0]})
    for i, c in enumerate(backward):
        pl.semaphore_wait(present.at[i], 1)
        c.start()
    pl.when(me == 0)(near_copy.start)

    for b in range(blocks):
        span = slice(b * BLOCK, (b + 1) * BLOCK)
        p = dot(design, xe[:samples, span], NN)
        high = p.astype(BF16).astype(F32)
        xe[samples:, span] = jnp.concatenate([high, p - high], 0).astype(BF16)

    gram_copy.wait()
    for name in ("prior", "levels", "dead"):
        loads[name].wait()
    lanes = lax.broadcasted_iota(jnp.int32, (8, 128), 1)
    subs = lax.broadcasted_iota(jnp.int32, (8, 128), 0)
    aug = gram_mine[...] + gram_theirs[...] + jnp.where(lanes == subs + 8, 1.0, 0.0)
    for k in range(DESIGN):
        row = aug[k : k + 1, :] / aug[k : k + 1, k : k + 1]
        aug = jnp.where(subs == k, row, aug - aug[:, k : k + 1] * row)
    diagonal = jnp.sum(jnp.where(lanes == subs + 8, aug, 0.0), 1, keepdims=True)
    inverse = [aug[:, 8 + k : 9 + k] for k in range(DESIGN)]
    weights = jnp.zeros(levels.shape, F32)
    for number in range(LEVELS + 1):
        weights = jnp.where(levels[...] == number, prior[number], weights)
    edge_weights = weights[:, BLOCK + 128 :]

    def shrink(m, s, weight):
        effects = inverse[0] * m[0:1]
        for k in range(1, DESIGN):
            effects = effects + inverse[k] * m[k : k + 1]
        left = jnp.sum(s, 0, keepdims=True) - jnp.sum(m * effects, 0, keepdims=True)
        noise = jnp.maximum(left, 0.0) / (total - DESIGN) + 1e-06
        squared = effects * effects
        return squared * effects / (squared + (noise * weight) * diagonal)

    def paired(shrunk):
        high = shrunk.astype(BF16).astype(F32)
        return jnp.concatenate([high, shrunk - high], 0).astype(BF16)

    def both(a, table, dims):
        return dot(a, table[0], dims) + dot(a, table[1], dims)

    def folded(res):
        return res[:8] + res[8:]

    def pick(a):
        return jnp.where(side == 0, a[:4], a[4:])

    only = jnp.where(lax.broadcasted_iota(jnp.int32, (8, samples), 0) == 0, 1.0, 0.0)
    only = only.astype(BF16)

    def summed(u, ref, skip=0):
        blank = [jnp.zeros((n, samples), F32) for n in (skip, 128 - skip - u.shape[0])]
        u = jnp.concatenate([*blank[:1], u, blank[1]] if skip else [u, blank[1]], 0)
        uh, ul = halves(u)
        sh, sl = halves(u * u)
        ref[0:8] = dot(design, uh, NT) + dot(design, ul, NT)
        ref[8:16] = dot(only, sh, NT) + dot(only, sl, NT)

    def shrunk_edge(mine, theirs):
        total_edge = mine[...] + theirs[...]
        return shrink(total_edge[0:8], total_edge[8:16], edge_weights)

    a_copy = copy(9, a_mine, a_theirs, {"sample": 1 - side})
    b_copy = copy(10, b_mine, b_theirs, {"sample": 1 - side})
    su_copy = copy(11, su_ref, su_got, {"genome": before[0]})
    w_copy = copy(13, w_mine, w_theirs, {"sample": 1 - side})

    def sum_before():
        forward[0].wait()
        forward[1].wait()
        summed(jnp.concatenate([rows[120:152] + got_e[...], rows[152:168] + got_m[0:16]], 0), a_mine)
        a_copy.start()

    def shrink_before():
        a_copy.wait()
        su_ref[...] = shrunk_edge(a_mine, a_theirs)

    pl.when(me > 0)(sum_before)

    for name in ("table_e", "wide"):
        loads[name].wait()
    e = dot3(a4, (table_e[0], table_e[1]), NN)
    eh, el = halves(e)
    stats_mine[0:8, width - 128 : width] = dot(design, eh, NN) + dot(design, el, NN)
    stats_mine[8:16, width - 128 : width] = jnp.sum((e * e).reshape(samples // 8, 8, 128), 0)
    for b in range(blocks):
        if b == 4:

            @pl.when(me > 0)
            def _():
                shrink_before()
                su_copy.start()

        depth = BLOCK + 128 if b < blocks - 1 else BLOCK
        span = slice(b * BLOCK, (b + 1) * BLOCK)
        window = xe[:, b * BLOCK : b * BLOCK + depth]
        res = dot(window, wide[0, :depth], NN) + dot(window, wide[1, :depth], NN)
        main = res[:samples]
        stats_mine[0:8, span] = res[samples : samples + 8] + res[samples + 8 :]
        stats_mine[8:16, span] = jnp.sum((main * main).reshape(samples // 8, 8, BLOCK), 0)
    stats_copy = copy(5, stats_mine, stats_theirs, {"sample": 1 - side})
    stats_copy.start()

    stats_copy.wait()
    lane = lax.broadcasted_iota(jnp.int32, (8, BLOCK), 1)
    coarse = (lane >= 128) & (lane < 144)
    for b in range(blocks):
        span = slice(b * BLOCK, (b + 1) * BLOCK)
        m = stats_mine[0:8, span] + stats_theirs[0:8, span]
        s = stats_mine[8:16, span] + stats_theirs[8:16, span]
        g = jnp.where(coarse, 0.0, shrink(m, s, weights[:, :BLOCK]))
        if b == blocks - 1:
            g = jnp.where(dead[...] > 0, 0.0, g)
        stack[16 * b : 16 * b + 16, :] = paired(g)
    span = slice(width - 128, width)
    m = stats_mine[0:8, span] + stats_theirs[0:8, span]
    s = stats_mine[8:16, span] + stats_theirs[8:16, span]
    se = paired(shrink(m, s, weights[:, BLOCK : BLOCK + 128]))
    y_main[...] = both(stack[...], (wide[0], wide[1]), NT)
    a4_main[...] = both(se, (table_e[0], table_e[1]), NT)

    for c in backward + forward[2:]:
        c.wait()
    pl.when(me == 0)(sum_before)
    u = rows[56:72] + got_m[16:32] + got_2[...] + back_1[0:16]
    u = jnp.concatenate(
        [
            u[0:8] + back_2[0:8],
            u[8:16] + got_3[...],
            rows[112:120] + back_1[16:24] + back_2[8:16] + back_3[...],
        ],
        0,
    )
    summed(u, b_mine, 48)
    b_copy.start()

    @pl.when(me == peers - 1)
    def _():
        near_copy.wait_recv()
        summed(jnp.concatenate([own_e[...] + near[0:32], rows[0:16] + near[32:48]], 0), w_mine)
        w_copy.start()
        w_copy.wait()
        su_got[...] = shrunk_edge(w_mine, w_theirs)

    pl.when(me < peers - 1)(su_copy.wait_recv)
    su = paired(su_got[...])
    a4 = folded(a4_main[...] + both(su[:, 32:48], (edge_cells[0, :16], edge_cells[1, :16]), NN))
    tail = folded(both(su[:, :32], (edge_last[0], edge_last[1]), NN))
    narrow = lax.broadcasted_iota(jnp.int32, (8, 128), 1) < 16
    for b in range(blocks):
        moved = a4 if b == 0 else pltpu.roll(a4, 128 - 16 * b, 1)
        stack[16 * b : 16 * b + 16, :128] = paired(jnp.where(narrow, moved, 0.0))
    y = y_main[...] + both(stack[:, :128], (wide[0, :, 128:256], wide[1, :, 128:256]), NT)
    begin = jnp.zeros((8, 128), F32)
    for b in range(blocks):
        piece = folded(y[16 * b : 16 * b + 16])
        parts = [piece[:, :128] + begin, piece[:, 128:256]]
        for h in range(2):
            at = b * BLOCK + h * 128
            if at >= length - TAIL:
                parts[h] = parts[h] + tail[:, at - length + TAIL : at - length + TAIL + 128]
            y_ref[:, at : at + 128] = pick(parts[h])
        begin = piece[:, 256:]

    loads["direct"].wait()
    pl.when(me == 0)(shrink_before)
    b_copy.wait()
    su = pick(su_ref[...] + shrunk_edge(b_mine, b_theirs))
    last = both(paired(su)[:, :80], (direct[0], direct[1]), NN)
    out[...] = y_ref[...] + last[:4] + last[4:]
    pl.when(me > 0)(su_copy.wait_send)
    pl.when(me == 0)(near_copy.wait_send)


def local(signal, coverage, design_codes, level_prior):
    samples, length = signal.shape
    blocks = length // BLOCK
    *pairs, l_main, l_e, l_u, straddles = tables(length)
    pieces = [jnp.asarray(two(t)) for t in pairs]
    levels = jnp.asarray(np.concatenate([l_main, l_e, l_u])[None])
    dead = jnp.asarray(straddles.astype(np.int32)[None])
    total = samples * lax.axis_size("sample")
    width = blocks * BLOCK + 128
    operands = (signal, coverage, design_codes, level_prior, levels, dead, *pieces)
    places = [pltpu.VMEM(a.shape, a.dtype) for a in operands]
    places[3] = pltpu.SMEM(level_prior.shape, F32)
    copies = 14
    return pl.pallas_call(
        functools.partial(kernel, total),
        out_shape=pltpu.VMEM((DESIGN // lax.axis_size("sample"), length), F32),
        in_specs=[pl.BlockSpec(memory_space=pltpu.HBM)] * len(operands),
        out_specs=pl.BlockSpec(memory_space=pltpu.VMEM),
        scratch_shapes=places
        + [
            pltpu.VMEM((8, samples), F32),
            pltpu.VMEM((samples + 16, length), BF16),
            pltpu.VMEM((length, 256), BF16),
            pltpu.VMEM((32, samples), F32),
            pltpu.VMEM((176, samples), F32),
            pltpu.VMEM((32, samples), F32),
            pltpu.VMEM((32, samples), F32),
            pltpu.VMEM((16, samples), F32),
            pltpu.VMEM((8, samples), F32),
            pltpu.VMEM((24, samples), F32),
            pltpu.VMEM((16, samples), F32),
            pltpu.VMEM((8, samples), F32),
            pltpu.VMEM((8, 128), F32),
            pltpu.VMEM((8, 128), F32),
            pltpu.VMEM((16, width), F32),
            pltpu.VMEM((16, width), F32),
            pltpu.VMEM((48, samples), F32),
            pltpu.VMEM((16, 128), F32),
            pltpu.VMEM((16, 128), F32),
            pltpu.VMEM((16, 128), F32),
            pltpu.VMEM((16, 128), F32),
            pltpu.VMEM((16, 128), F32),
            pltpu.VMEM((16, 128), F32),
            pltpu.VMEM((8, 128), F32),
            pltpu.VMEM((8, 128), F32),
            pltpu.VMEM((16 * blocks, BLOCK), BF16),
            pltpu.VMEM((4, length), F32),
            pltpu.VMEM((16 * blocks, BLOCK + 128), F32),
            pltpu.VMEM((16, 128), F32),
            pltpu.SemaphoreType.DMA((11 + 2 * (length // CHUNK),)),
            pltpu.SemaphoreType.DMA((copies,)),
            pltpu.SemaphoreType.DMA((copies,)),
            pltpu.SemaphoreType.REGULAR((3,)),
        ],
        compiler_params=pltpu.CompilerParams(
            collective_id=0, has_side_effects=True, vmem_limit_bytes=56 * 2**20
        ),
    )(*operands)


def solution(mesh):
    placed = (
        P("sample", ("parts", "genome")),
        P("sample", ("parts", "genome")),
        P(None, "sample"),
        P(),
    )
    return jax.shard_map(
        local,
        mesh=mesh,
        in_specs=placed,
        out_specs=P("sample", ("parts", "genome")),
        check_vma=False,
    )
```

```python
import functools

import jax
import jax.numpy as jnp
import ml_dtypes
import numpy as np
from jax import lax
from jax.experimental import pallas as pl
from jax.experimental.pallas import tpu as pltpu
from jax.sharding import PartitionSpec as P

LEVELS = 10
DESIGN = 8
FINE = 4
BLOCK = 256
TAIL = 512
LOWPASS = np.array(
    (
        0.23037781330885523,
        0.7148465705525415,
        0.6308807679295904,
        -0.02798376941698385,
        -0.18703481171888114,
        0.030841381835986965,
        0.032883011666982945,
        -0.010597401784997278,
    )
)
HIGHPASS = np.array([(-1.0) ** m * LOWPASS[7 - m] for m in range(8)])


def spread(taps, step):
    out = np.zeros(7 * step + 1)
    out[::step] = taps
    return out


def composite(levels):
    low = np.ones(1)
    details = []
    for j in range(levels):
        details.append(np.convolve(low, spread(HIGHPASS, 2**j)))
        low = np.convolve(low, spread(LOWPASS, 2**j))
    return details, low


def column(taps, start, size):
    out = np.zeros(size)
    for i, tap in enumerate(taps):
        if 0 <= start + i < size:
            out[start + i] = tap
    return out


def tables(length):
    det, low = composite(LEVELS)
    fine_low = composite(FINE)[1]
    coarse_det, coarse_low = composite(LEVELS - FINE)
    cells = length >> FINE
    group1 = [(1, k) for k in range(125)] + [(2, k) for k in range(3)]
    group2 = [(0, k) for k in range(16)] + [(4, k) for k in range(16)] + [(3, k) for k in range(32)]
    group2 += [(2, k) for k in range(3, 64)] + [(1, k) for k in range(125, 128)]
    wide = np.zeros((BLOCK + 128, 2 * 128))
    level_main = np.zeros(256, np.int32)
    straddles = np.zeros(256, bool)
    for c, (level, k) in enumerate(group1 + group2):
        taps = det[level - 1] if level else fine_low
        step = 2 ** (level or FINE)
        wide[:, c] = column(taps, step * k, BLOCK + 128)
        level_main[c] = (level or 1) - 1
        straddles[c] = level > 0 and step * k + len(taps) > BLOCK
    coarse = [(level, k) for level in range(FINE + 1, LEVELS + 1) for k in range(length >> level)]
    coarse += [(0, k) for k in range(length >> LEVELS)]
    table_e = np.zeros((cells, 128))
    level_e = np.zeros(128, np.int32)
    for c, (level, k) in enumerate(coarse):
        taps = coarse_det[level - FINE - 1] if level else coarse_low
        step = 2 ** ((level or LEVELS) - FINE)
        level_e[c] = level - 1 if level else LEVELS
        full = det[level - 1] if level else low
        if (step << FINE) * k + len(full) <= length:
            table_e[:, c] = column(taps, step * k, cells)
    edge = []
    for level in range(1, LEVELS + 1):
        size = length >> level
        first = -(-(length - len(det[level - 1]) + 1) // 2**level)
        edge += [(level, k) for k in range(max(first, 0), size)]
    early = [e for e in edge if e[0] < 7]
    middle = [e for e in edge if 7 <= e[0] < 9 or (e[0] == 9 and e[1] < 2)]
    late = [e for e in edge if e not in early + middle] + [(0, k) for k in range(length >> LEVELS)]
    early += [None] * (32 - len(early))
    middle += [None] * (16 - len(middle))
    late += [None] * (8 - len(late))
    coarsest = late[2:6]
    none = [None] * 2
    sets = [row for row in late if row]
    levels = np.zeros(128, np.int32)
    for r, row in enumerate(early + middle + sets + sets + coarsest + late):
        if row:
            levels[r] = row[0] - 1 if row[0] else LEVELS
    shifted = []
    for shift, part in (
        (0, middle + sets), (1, sets), (2, coarsest),
        (0, 3 * none + sets), (1, coarsest),
        (0, 2 * none + coarsest),
        (1, sets), (2, sets), (3, coarsest),
        (2, sets), (3, sets), (0, 2 * none), (1, late),
        (3, late), (2, late),
        (0, late),
        (1, early + middle),
    ):
        shifted += [(row, shift * length) for row in part]
    edge_cells = np.zeros((176, cells))
    edge_first = np.zeros((176, 128))
    edge_last = np.zeros((32, TAIL))
    direct = np.zeros((80, length))
    into = {**{120 + r: r for r in range(48)}, **{56 + r: 48 + r for r in range(16)}, **{112 + r: 64 + r for r in range(8)}}
    for r, (row, shift) in enumerate(shifted):
        if row is None:
            continue
        level, k = row
        if r in into:
            full = det[level - 1] if level else low
            direct[into[r]] = column(full, k * 2 ** (level or LEVELS) - shift, length)
        if 1 <= level <= FINE:
            edge_first[r] = column(det[level - 1], k * 2**level - shift, 128)
            continue
        taps = coarse_det[level - FINE - 1] if level else coarse_low
        start = k * 2 ** ((level or LEVELS) - FINE) - (shift >> FINE)
        edge_cells[r] = column(taps, start, cells)
        for c in range(-6, 0):
            if 0 <= c - start < len(taps):
                edge_first[r] += taps[c - start] * column(fine_low, c * 2**FINE, 128)
    for r, row in enumerate(early):
        if row:
            edge_last[r] = column(det[row[0] - 1], row[1] * 2 ** row[0] - (length - TAIL), TAIL)
    base = np.stack([column(fine_low, (k if k < 16 else k - 128) * 2**FINE, BLOCK) for k in range(128)], 1)
    return base, wide, table_e, edge_cells, edge_first, edge_last, direct, level_main, level_e, levels, straddles


def two(table):
    high = table.astype(np.float32).astype(ml_dtypes.bfloat16)
    rest = (table - high.astype(np.float64)).astype(np.float32).astype(ml_dtypes.bfloat16)
    return np.stack([high, rest])


NN = (((1,), (0,)), ((), ()))
NT = (((1,), (1,)), ((), ()))


def dot(a, b, dims):
    return lax.dot_general(a, b, dims, preferred_element_type=jnp.float32)


def halves(a):
    high = a.astype(jnp.bfloat16)
    return high, (a - high.astype(jnp.float32)).astype(jnp.bfloat16)


def dot3(a, b, dims):
    return dot(a[0], b[0], dims) + dot(a[0], b[1], dims) + dot(a[1], b[0], dims)


CHUNK = 512
F32 = jnp.float32
BF16 = jnp.bfloat16


def kernel(total, *refs):
    inputs = refs[:13]
    out = refs[13]
    loaded = refs[14:27]
    (
        d_ref,
        xe,
        dense,
        own_e,
        rows,
        got_e,
        got_m,
        got_2,
        got_3,
        back_1,
        back_2,
        back_3,
        gram_mine,
        gram_theirs,
        stats_mine,
        stats_theirs,
        near,
        a_mine,
        a_theirs,
        b_mine,
        b_theirs,
        w_mine,
        w_theirs,
        su_ref,
        su_got,
        stack,
        y_ref,
        y_main,
        a4_main,
        load_sem,
        send_sem,
        recv_sem,
        present,
    ) = refs[27:]
    signal, coverage = loaded[:2]
    codes, prior, levels, dead, base, wide, table_e, edge_cells, edge_first, edge_last, direct = loaded[2:]
    samples, length = signal.shape
    blocks = length // BLOCK
    chunks = length // CHUNK
    width = blocks * BLOCK + 128
    me = lax.axis_index("genome")
    peers = lax.axis_size("genome")
    side = lax.axis_index("sample")
    before = [lax.rem(me + peers - i, peers) for i in (1, 2, 3)]
    after = [lax.rem(me + i, peers) for i in (1, 2, 3)]

    barrier = pltpu.get_barrier_semaphore()
    for peer in before:
        pl.semaphore_signal(barrier, inc=1, device_id={"genome": peer})
    pl.semaphore_signal(barrier, inc=1, device_id={"sample": 1 - side})

    loads = {}

    def load(name, src, dst):
        c = pltpu.make_async_copy(src, dst, load_sem.at[len(loads)])
        c.start()
        loads[name] = c

    def load_chunk(i):
        span = pl.ds(i * CHUNK, CHUNK)
        load(("signal", i), inputs[0].at[:, span], signal.at[:, span])
        load(("coverage", i), inputs[1].at[:, span], coverage.at[:, span])

    names = ("codes", "prior", "levels", "dead", "base", "wide", "table_e", "cells", "first", "last", "direct")
    later = dict(zip(names, zip(inputs[2:], loaded[2:])))
    order = [chunks - 1, *range(chunks - 1)]
    load("base", *later["base"])
    load("codes", *later["codes"])
    load_chunk(order[0])
    load("last", *later["last"])
    load_chunk(order[1])
    load("first", *later["first"])
    for i in order[2:]:
        load_chunk(i)
    load("cells", *later["cells"])

    def copy(number, src, dst, device):
        return pltpu.make_async_remote_copy(
            src_ref=src,
            dst_ref=dst,
            send_sem=send_sem.at[number],
            recv_sem=recv_sem.at[number],
            device_id=device,
            device_id_type=pl.DeviceIdType.MESH,
        )

    loads["codes"].wait()
    d_ref[0:1, :] = jnp.ones((1, samples), F32)
    d_ref[1:8, :] = codes[...].astype(F32) - 2.0
    design = d_ref[...].astype(BF16)
    padded = jnp.concatenate([d_ref[...], jnp.zeros((120, samples), F32)], 0)
    gram_mine[...] = dot(design, padded.astype(BF16), NT)
    loads["base"].wait()
    for half in range(2):
        part = base[half].astype(F32)
        lane = lax.broadcasted_iota(jnp.int32, part.shape, 1)
        for b in range(blocks):
            moved = jnp.where(lane < 16, part, 0.0) if b == 0 else pltpu.roll(part, 16 * b, 1)
            dense[b * BLOCK : (b + 1) * BLOCK, half * 128 : half * 128 + 128] = moved.astype(BF16)

    def enter():
        pl.semaphore_wait(barrier, 4)
        for i, peer in enumerate(after):
            pl.semaphore_signal(present.at[i], inc=1, device_id={"genome": peer})

    def send_last():
        forward[0].start()
        gram_copy.start()

    forward = [copy(0, own_e, got_e, {"genome": after[0]})]
    gram_copy = copy(1, gram_mine, gram_theirs, {"sample": 1 - side})
    pl.when(me >= peers // 2)(enter)
    a4 = None
    for i in order:
        loads["signal", i].wait()
        loads["coverage", i].wait()
        span = slice(i * CHUNK, (i + 1) * CHUNK)
        x = (signal[:, span].astype(F32) * coverage[:, span].astype(F32)).astype(BF16)
        xe[:samples, span] = x
        if i == chunks - 1:
            loads["last"].wait()
            own_e[...] = dot(edge_last[0], x, NT) + dot(edge_last[1], x, NT)
            pl.when(me >= peers // 2)(send_last)
        if i == 0:
            loads["first"].wait()
            first = dot(edge_first[0], x[:, :128], NT) + dot(edge_first[1], x[:, :128], NT)
        piece = dot(x, dense[span], NN)
        a4 = piece if a4 is None else a4 + piece
    a4 = halves(a4[:, :128] + a4[:, 128:])

    @pl.when(me < peers // 2)
    def _():
        enter()
        send_last()


    loads["cells"].wait()
    rows[0:64] = dot3((edge_cells[0, 0:64], edge_cells[1, 0:64]), a4, NT) + first[0:64]
    forward += [
        copy(2, rows.at[0:32], got_m, {"genome": after[0]}),
        copy(3, rows.at[32:48], got_2, {"genome": after[1]}),
        copy(4, rows.at[48:56], got_3, {"genome": after[2]}),
    ]
    for c in forward[1:]:
        c.start()
    for name in ("table_e", "wide", "prior", "levels", "dead", "direct"):
        load(name, *later[name])
    rows[64:176] = dot3((edge_cells[0, 64:176], edge_cells[1, 64:176]), a4, NT) + first[64:176]
    backward = [
        copy(6, rows.at[72:96], back_1, {"genome": before[0]}),
        copy(7, rows.at[96:112], back_2, {"genome": before[1]}),
        copy(8, rows.at[96:104], back_3, {"genome": before[2]}),
    ]
    near_copy = copy(12, rows.at[120:168], near, {"genome": before[0]})
    for i, c in enumerate(backward):
        pl.semaphore_wait(present.at[i], 1)
        c.start()
    pl.when(me == 0)(near_copy.start)

    for b in range(blocks):
        span = slice(b * BLOCK, (b + 1) * BLOCK)
        p = dot(design, xe[:samples, span], NN)
        high = p.astype(BF16).astype(F32)
        xe[samples:, span] = jnp.concatenate([high, p - high], 0).astype(BF16)

    gram_copy.wait()
    for name in ("prior", "levels", "dead"):
        loads[name].wait()
    lanes = lax.broadcasted_iota(jnp.int32, (8, 128), 1)
    subs = lax.broadcasted_iota(jnp.int32, (8, 128), 0)
    aug = gram_mine[...] + gram_theirs[...] + jnp.where(lanes == subs + 8, 1.0, 0.0)
    for k in range(DESIGN):
        row = aug[k : k + 1, :] / aug[k : k + 1, k : k + 1]
        aug = jnp.where(subs == k, row, aug - aug[:, k : k + 1] * row)
    diagonal = jnp.sum(jnp.where(lanes == subs + 8, aug, 0.0), 1, keepdims=True)
    inverse = [aug[:, 8 + k : 9 + k] for k in range(DESIGN)]
    weights = jnp.zeros(levels.shape, F32)
    for number in range(LEVELS + 1):
        weights = jnp.where(levels[...] == number, prior[number], weights)
    edge_weights = weights[:, BLOCK + 128 :]

    def shrink(m, s, weight):
        effects = inverse[0] * m[0:1]
        for k in range(1, DESIGN):
            effects = effects + inverse[k] * m[k : k + 1]
        left = jnp.sum(s, 0, keepdims=True) - jnp.sum(m * effects, 0, keepdims=True)
        noise = jnp.maximum(left, 0.0) / (total - DESIGN) + 1e-06
        squared = effects * effects
        return squared * effects / (squared + (noise * weight) * diagonal)

    def paired(shrunk):
        high = shrunk.astype(BF16).astype(F32)
        return jnp.concatenate([high, shrunk - high], 0).astype(BF16)

    def both(a, table, dims):
        return dot(a, table[0], dims) + dot(a, table[1], dims)

    def folded(res):
        return res[:8] + res[8:]

    def pick(a):
        return jnp.where(side == 0, a[:4], a[4:])

    only = jnp.where(lax.broadcasted_iota(jnp.int32, (8, 128), 0) == 0, 1.0, 0.0)
    only = only.astype(BF16)

    def summed(u, ref, skip=0):
        blank = [jnp.zeros((n, samples), F32) for n in (skip, 128 - skip - u.shape[0])]
        u = jnp.concatenate([*blank[:1], u, blank[1]] if skip else [u, blank[1]], 0)
        uh, ul = halves(u)
        squares = u * u
        sh, sl = halves(sum(squares[:, i : i + 128] for i in range(0, samples, 128)))
        ref[0:8] = dot(design, uh, NT) + dot(design, ul, NT)
        ref[8:16] = dot(only, sh, NT) + dot(only, sl, NT)

    def shrunk_edge(mine, theirs):
        total_edge = mine[...] + theirs[...]
        return shrink(total_edge[0:8], total_edge[8:16], edge_weights)

    a_copy = copy(9, a_mine, a_theirs, {"sample": 1 - side})
    b_copy = copy(10, b_mine, b_theirs, {"sample": 1 - side})
    su_copy = copy(11, su_ref, su_got, {"genome": before[0]})
    w_copy = copy(13, w_mine, w_theirs, {"sample": 1 - side})

    def u_before():
        return jnp.concatenate([rows[120:152] + got_e[...], rows[152:168] + got_m[0:16]], 0)

    def sum_before():
        forward[0].wait()
        forward[1].wait()
        summed(u_before(), a_mine)
        a_copy.start()

    def shrink_before():
        a_copy.wait()
        su_ref[...] = shrunk_edge(a_mine, a_theirs)

    def give_back():
        shrink_before()
        su_copy.start()

    pl.when(me == 1)(sum_before)
    for name in ("table_e", "wide"):
        loads[name].wait()
    e = dot3(a4, (table_e[0], table_e[1]), NN)
    eh, el = halves(e)
    stats_mine[0:8, width - 128 : width] = dot(design, eh, NN) + dot(design, el, NN)
    stats_mine[8:16, width - 128 : width] = jnp.sum((e * e).reshape(samples // 8, 8, 128), 0)
    for b in range(blocks):
        if b == 2:
            pl.when(me == 1)(give_back)
        depth = BLOCK + 128 if b < blocks - 1 else BLOCK
        span = slice(b * BLOCK, (b + 1) * BLOCK)
        window = xe[:, b * BLOCK : b * BLOCK + depth]
        res = dot(window, wide[0, :depth], NN) + dot(window, wide[1, :depth], NN)
        main = res[:samples]
        stats_mine[0:8, span] = res[samples : samples + 8] + res[samples + 8 :]
        stats_mine[8:16, span] = jnp.sum((main * main).reshape(samples // 8, 8, BLOCK), 0)
    stats_copy = copy(5, stats_mine, stats_theirs, {"sample": 1 - side})
    stats_copy.start()

    pl.when(me > 1)(sum_before)

    stats_copy.wait()
    lane = lax.broadcasted_iota(jnp.int32, (8, BLOCK), 1)
    coarse = (lane >= 128) & (lane < 144)
    for b in range(blocks):
        span = slice(b * BLOCK, (b + 1) * BLOCK)
        m = stats_mine[0:8, span] + stats_theirs[0:8, span]
        s = stats_mine[8:16, span] + stats_theirs[8:16, span]
        g = jnp.where(coarse, 0.0, shrink(m, s, weights[:, :BLOCK]))
        if b == blocks - 1:
            g = jnp.where(dead[...] > 0, 0.0, g)
        stack[16 * b : 16 * b + 16, :] = paired(g)
    span = slice(width - 128, width)
    m = stats_mine[0:8, span] + stats_theirs[0:8, span]
    s = stats_mine[8:16, span] + stats_theirs[8:16, span]
    se = paired(shrink(m, s, weights[:, BLOCK : BLOCK + 128]))
    pl.when(me > 1)(give_back)

    y_main[...] = both(stack[...], (wide[0], wide[1]), NT)
    a4_main[...] = both(se, (table_e[0], table_e[1]), NT)

    for c in backward + forward[2:]:
        c.wait()

    def u_long():
        u = rows[56:72] + got_m[16:32] + got_2[...] + back_1[0:16]
        return jnp.concatenate(
            [
                u[0:8] + back_2[0:8],
                u[8:16] + got_3[...],
                rows[112:120] + back_1[16:24] + back_2[8:16] + back_3[...],
            ],
            0,
        )

    @pl.when(me == 0)
    def _():
        forward[0].wait()
        forward[1].wait()
        summed(jnp.concatenate([u_before(), u_long()], 0), b_mine)
        su_ref[...] = jnp.zeros(su_ref.shape, F32)

    @pl.when(me > 0)
    def _():
        summed(u_long(), b_mine, 48)

    b_copy.start()

    @pl.when(me == peers - 1)
    def _():
        near_copy.wait_recv()
        summed(jnp.concatenate([own_e[...] + near[0:32], rows[0:16] + near[32:48]], 0), w_mine)
        w_copy.start()
        w_copy.wait()
        su_got[...] = shrunk_edge(w_mine, w_theirs)

    pl.when(me < peers - 1)(su_copy.wait_recv)
    su = paired(su_got[...])
    a4 = folded(a4_main[...] + both(su[:, 32:48], (edge_cells[0, :16], edge_cells[1, :16]), NN))
    tail = folded(both(su[:, :32], (edge_last[0], edge_last[1]), NN))
    narrow = lax.broadcasted_iota(jnp.int32, (8, 128), 1) < 16
    for b in range(blocks):
        moved = a4 if b == 0 else pltpu.roll(a4, 128 - 16 * b, 1)
        stack[16 * b : 16 * b + 16, :128] = paired(jnp.where(narrow, moved, 0.0))
    y = y_main[...] + both(stack[:, :128], (wide[0, :, 128:256], wide[1, :, 128:256]), NT)
    begin = jnp.zeros((8, 128), F32)
    for b in range(blocks):
        piece = folded(y[16 * b : 16 * b + 16])
        parts = [piece[:, :128] + begin, piece[:, 128:256]]
        for h in range(2):
            at = b * BLOCK + h * 128
            if at >= length - TAIL:
                parts[h] = parts[h] + tail[:, at - length + TAIL : at - length + TAIL + 128]
            y_ref[:, at : at + 128] = pick(parts[h])
        begin = piece[:, 256:]

    loads["direct"].wait()
    b_copy.wait()
    su = pick(su_ref[...] + shrunk_edge(b_mine, b_theirs))
    last = both(paired(su)[:, :80], (direct[0], direct[1]), NN)
    out[...] = y_ref[...] + last[:4] + last[4:]
    pl.when(me > 0)(su_copy.wait_send)
    pl.when(me == 0)(near_copy.wait_send)


def local(signal, coverage, design_codes, level_prior):
    samples, length = signal.shape
    blocks = length // BLOCK
    *pairs, l_main, l_e, l_u, straddles = tables(length)
    pieces = [jnp.asarray(two(t)) for t in pairs]
    levels = jnp.asarray(np.concatenate([l_main, l_e, l_u])[None])
    dead = jnp.asarray(straddles.astype(np.int32)[None])
    total = samples * lax.axis_size("sample")
    width = blocks * BLOCK + 128
    operands = (signal, coverage, design_codes, level_prior, levels, dead, *pieces)
    places = [pltpu.VMEM(a.shape, a.dtype) for a in operands]
    places[3] = pltpu.SMEM(level_prior.shape, F32)
    copies = 14
    return pl.pallas_call(
        functools.partial(kernel, total),
        out_shape=pltpu.VMEM((DESIGN // lax.axis_size("sample"), length), F32),
        in_specs=[pl.BlockSpec(memory_space=pltpu.HBM)] * len(operands),
        out_specs=pl.BlockSpec(memory_space=pltpu.VMEM),
        scratch_shapes=places
        + [
            pltpu.VMEM((8, samples), F32),
            pltpu.VMEM((samples + 16, length), BF16),
            pltpu.VMEM((length, 256), BF16),
            pltpu.VMEM((32, samples), F32),
            pltpu.VMEM((176, samples), F32),
            pltpu.VMEM((32, samples), F32),
            pltpu.VMEM((32, samples), F32),
            pltpu.VMEM((16, samples), F32),
            pltpu.VMEM((8, samples), F32),
            pltpu.VMEM((24, samples), F32),
            pltpu.VMEM((16, samples), F32),
            pltpu.VMEM((8, samples), F32),
            pltpu.VMEM((8, 128), F32),
            pltpu.VMEM((8, 128), F32),
            pltpu.VMEM((16, width), F32),
            pltpu.VMEM((16, width), F32),
            pltpu.VMEM((48, samples), F32),
            pltpu.VMEM((16, 128), F32),
            pltpu.VMEM((16, 128), F32),
            pltpu.VMEM((16, 128), F32),
            pltpu.VMEM((16, 128), F32),
            pltpu.VMEM((16, 128), F32),
            pltpu.VMEM((16, 128), F32),
            pltpu.VMEM((8, 128), F32),
            pltpu.VMEM((8, 128), F32),
            pltpu.VMEM((16 * blocks, BLOCK), BF16),
            pltpu.VMEM((4, length), F32),
            pltpu.VMEM((16 * blocks, BLOCK + 128), F32),
            pltpu.VMEM((16, 128), F32),
            pltpu.SemaphoreType.DMA((11 + 2 * (length // CHUNK),)),
            pltpu.SemaphoreType.DMA((copies,)),
            pltpu.SemaphoreType.DMA((copies,)),
            pltpu.SemaphoreType.REGULAR((3,)),
        ],
        compiler_params=pltpu.CompilerParams(
            collective_id=0, has_side_effects=True, vmem_limit_bytes=56 * 2**20
        ),
    )(*operands)


def solution(mesh):
    placed = (
        P("sample", ("parts", "genome")),
        P("sample", ("parts", "genome")),
        P(None, "sample"),
        P(),
    )
    return jax.shard_map(
        local,
        mesh=mesh,
        in_specs=placed,
        out_specs=P("sample", ("parts", "genome")),
        check_vma=False,
    )
```

```python
import functools

import jax
import jax.numpy as jnp
import ml_dtypes
import numpy as np
from jax import lax
from jax.experimental import pallas as pl
from jax.experimental.pallas import tpu as pltpu
from jax.sharding import PartitionSpec as P

LEVELS = 10
DESIGN = 8
FINE = 4
BLOCK = 256
TAIL = 512
LOWPASS = np.array(
    (
        0.23037781330885523,
        0.7148465705525415,
        0.6308807679295904,
        -0.02798376941698385,
        -0.18703481171888114,
        0.030841381835986965,
        0.032883011666982945,
        -0.010597401784997278,
    )
)
HIGHPASS = np.array([(-1.0) ** m * LOWPASS[7 - m] for m in range(8)])


def spread(taps, step):
    out = np.zeros(7 * step + 1)
    out[::step] = taps
    return out


def composite(levels):
    low = np.ones(1)
    details = []
    for j in range(levels):
        details.append(np.convolve(low, spread(HIGHPASS, 2**j)))
        low = np.convolve(low, spread(LOWPASS, 2**j))
    return details, low


def column(taps, start, size):
    out = np.zeros(size)
    for i, tap in enumerate(taps):
        if 0 <= start + i < size:
            out[start + i] = tap
    return out


def tables(length):
    det, low = composite(LEVELS)
    fine_low = composite(FINE)[1]
    coarse_det, coarse_low = composite(LEVELS - FINE)
    cells = length >> FINE
    group1 = [(1, k) for k in range(125)] + [(2, k) for k in range(3)]
    group2 = [(0, k) for k in range(16)] + [(4, k) for k in range(16)] + [(3, k) for k in range(32)]
    group2 += [(2, k) for k in range(3, 64)] + [(1, k) for k in range(125, 128)]
    wide = np.zeros((BLOCK + 128, 2 * 128))
    level_main = np.zeros(256, np.int32)
    straddles = np.zeros(256, bool)
    for c, (level, k) in enumerate(group1 + group2):
        taps = det[level - 1] if level else fine_low
        step = 2 ** (level or FINE)
        wide[:, c] = column(taps, step * k, BLOCK + 128)
        level_main[c] = (level or 1) - 1
        straddles[c] = level > 0 and step * k + len(taps) > BLOCK
    coarse = [(level, k) for level in range(FINE + 1, LEVELS + 1) for k in range(length >> level)]
    coarse += [(0, k) for k in range(length >> LEVELS)]
    table_e = np.zeros((cells, 128))
    level_e = np.zeros(128, np.int32)
    for c, (level, k) in enumerate(coarse):
        taps = coarse_det[level - FINE - 1] if level else coarse_low
        step = 2 ** ((level or LEVELS) - FINE)
        level_e[c] = level - 1 if level else LEVELS
        full = det[level - 1] if level else low
        if (step << FINE) * k + len(full) <= length:
            table_e[:, c] = column(taps, step * k, cells)
    edge = []
    for level in range(1, LEVELS + 1):
        size = length >> level
        first = -(-(length - len(det[level - 1]) + 1) // 2**level)
        edge += [(level, k) for k in range(max(first, 0), size)]
    early = [e for e in edge if e[0] < 7]
    middle = [e for e in edge if 7 <= e[0] < 9 or (e[0] == 9 and e[1] < 2)]
    late = [e for e in edge if e not in early + middle] + [(0, k) for k in range(length >> LEVELS)]
    early += [None] * (32 - len(early))
    middle += [None] * (16 - len(middle))
    late += [None] * (8 - len(late))
    coarsest = late[2:6]
    none = [None] * 2
    sets = [row for row in late if row]
    levels = np.zeros(128, np.int32)
    for r, row in enumerate(early + middle + sets + sets + coarsest + late):
        if row:
            levels[r] = row[0] - 1 if row[0] else LEVELS
    shifted = []
    for shift, part in (
        (0, middle + sets), (1, sets), (2, coarsest),
        (0, 3 * none + sets), (1, coarsest),
        (0, 2 * none + coarsest),
        (1, sets), (2, sets), (3, coarsest),
        (2, sets), (3, sets), (0, 2 * none), (1, late),
        (3, late), (2, late),
        (0, late),
        (1, early + middle),
    ):
        shifted += [(row, shift * length) for row in part]
    edge_cells = np.zeros((176, cells))
    edge_first = np.zeros((176, 128))
    edge_last = np.zeros((32, TAIL))
    direct = np.zeros((128, length))
    into = {**{120 + r: r for r in range(48)}, **{56 + r: 48 + r for r in range(16)}, **{112 + r: 64 + r for r in range(8)}}
    for r, (row, shift) in enumerate(shifted):
        if row is None:
            continue
        level, k = row
        if r in into:
            full = det[level - 1] if level else low
            direct[into[r]] = column(full, k * 2 ** (level or LEVELS) - shift, length)
        if 1 <= level <= FINE:
            edge_first[r] = column(det[level - 1], k * 2**level - shift, 128)
            continue
        taps = coarse_det[level - FINE - 1] if level else coarse_low
        start = k * 2 ** ((level or LEVELS) - FINE) - (shift >> FINE)
        edge_cells[r] = column(taps, start, cells)
        for c in range(-6, 0):
            if 0 <= c - start < len(taps):
                edge_first[r] += taps[c - start] * column(fine_low, c * 2**FINE, 128)
    for r, row in enumerate(early + middle):
        if row:
            direct[80 + r] = column(det[row[0] - 1], row[1] * 2 ** row[0], length)
    for r, row in enumerate(early):
        if row:
            edge_last[r] = column(det[row[0] - 1], row[1] * 2 ** row[0] - (length - TAIL), TAIL)
    base = np.stack([column(fine_low, (k if k < 16 else k - 128) * 2**FINE, BLOCK) for k in range(128)], 1)
    return base, wide, table_e, edge_cells, edge_first, edge_last, direct, level_main, level_e, levels, straddles


def two(table):
    high = table.astype(np.float32).astype(ml_dtypes.bfloat16)
    rest = (table - high.astype(np.float64)).astype(np.float32).astype(ml_dtypes.bfloat16)
    return np.stack([high, rest])


NN = (((1,), (0,)), ((), ()))
NT = (((1,), (1,)), ((), ()))


def dot(a, b, dims):
    return lax.dot_general(a, b, dims, preferred_element_type=jnp.float32)


def halves(a):
    high = a.astype(jnp.bfloat16)
    return high, (a - high.astype(jnp.float32)).astype(jnp.bfloat16)


def dot3(a, b, dims):
    return dot(a[0], b[0], dims) + dot(a[0], b[1], dims) + dot(a[1], b[0], dims)


CHUNK = 512
F32 = jnp.float32
BF16 = jnp.bfloat16


def kernel(total, *refs):
    inputs = refs[:13]
    out = refs[13]
    loaded = refs[14:27]
    (
        d_ref,
        xe,
        dense,
        own_e,
        rows,
        got_e,
        got_m,
        got_2,
        got_3,
        back_1,
        back_2,
        back_3,
        gram_mine,
        gram_theirs,
        stats_mine,
        stats_theirs,
        near,
        a_mine,
        a_theirs,
        b_mine,
        b_theirs,
        w_mine,
        w_theirs,
        su_ref,
        su_got,
        stack,
        y_ref,
        y_main,
        a4_main,
        load_sem,
        send_sem,
        recv_sem,
        present,
    ) = refs[27:]
    signal, coverage = loaded[:2]
    codes, prior, levels, dead, base, wide, table_e, edge_cells, edge_first, edge_last, direct = loaded[2:]
    samples, length = signal.shape
    blocks = length // BLOCK
    chunks = length // CHUNK
    width = blocks * BLOCK + 128
    me = lax.axis_index("genome")
    peers = lax.axis_size("genome")
    side = lax.axis_index("sample")
    before = [lax.rem(me + peers - i, peers) for i in (1, 2, 3)]
    after = [lax.rem(me + i, peers) for i in (1, 2, 3)]

    barrier = pltpu.get_barrier_semaphore()
    for peer in before:
        pl.semaphore_signal(barrier, inc=1, device_id={"genome": peer})
    pl.semaphore_signal(barrier, inc=1, device_id={"sample": 1 - side})

    loads = {}

    def load(name, src, dst):
        c = pltpu.make_async_copy(src, dst, load_sem.at[len(loads)])
        c.start()
        loads[name] = c

    def load_chunk(i):
        span = pl.ds(i * CHUNK, CHUNK)
        load(("signal", i), inputs[0].at[:, span], signal.at[:, span])
        load(("coverage", i), inputs[1].at[:, span], coverage.at[:, span])

    names = ("codes", "prior", "levels", "dead", "base", "wide", "table_e", "cells", "first", "last", "direct")
    later = dict(zip(names, zip(inputs[2:], loaded[2:])))
    order = [chunks - 1, *range(chunks - 1)]
    load("base", *later["base"])
    load("codes", *later["codes"])
    load_chunk(order[0])
    load("last", *later["last"])
    load_chunk(order[1])
    load("first", *later["first"])
    for i in order[2:]:
        load_chunk(i)
    load("cells", *later["cells"])

    def copy(number, src, dst, device):
        return pltpu.make_async_remote_copy(
            src_ref=src,
            dst_ref=dst,
            send_sem=send_sem.at[number],
            recv_sem=recv_sem.at[number],
            device_id=device,
            device_id_type=pl.DeviceIdType.MESH,
        )

    loads["codes"].wait()
    d_ref[0:1, :] = jnp.ones((1, samples), F32)
    d_ref[1:8, :] = codes[...].astype(F32) - 2.0
    design = d_ref[...].astype(BF16)
    padded = jnp.concatenate([d_ref[...], jnp.zeros((120, samples), F32)], 0)
    gram_mine[...] = dot(design, padded.astype(BF16), NT)
    loads["base"].wait()
    for half in range(2):
        part = base[half].astype(F32)
        lane = lax.broadcasted_iota(jnp.int32, part.shape, 1)
        for b in range(blocks):
            moved = jnp.where(lane < 16, part, 0.0) if b == 0 else pltpu.roll(part, 16 * b, 1)
            dense[b * BLOCK : (b + 1) * BLOCK, half * 128 : half * 128 + 128] = moved.astype(BF16)

    def enter():
        pl.semaphore_wait(barrier, 4)
        for i, peer in enumerate(after):
            pl.semaphore_signal(present.at[i], inc=1, device_id={"genome": peer})

    def send_last():
        forward[0].start()
        gram_copy.start()

    forward = [copy(0, own_e, got_e, {"genome": after[0]})]
    gram_copy = copy(1, gram_mine, gram_theirs, {"sample": 1 - side})
    pl.when(me >= peers // 2)(enter)
    a4 = None
    for i in order:
        loads["signal", i].wait()
        loads["coverage", i].wait()
        span = slice(i * CHUNK, (i + 1) * CHUNK)
        x = (signal[:, span].astype(F32) * coverage[:, span].astype(F32)).astype(BF16)
        xe[:samples, span] = x
        if i == chunks - 1:
            loads["last"].wait()
            own_e[...] = dot(edge_last[0], x, NT) + dot(edge_last[1], x, NT)
            pl.when(me >= peers // 2)(send_last)
        if i == 0:
            loads["first"].wait()
            first = dot(edge_first[0], x[:, :128], NT) + dot(edge_first[1], x[:, :128], NT)
        piece = dot(x, dense[span], NN)
        a4 = piece if a4 is None else a4 + piece
    a4 = halves(a4[:, :128] + a4[:, 128:])

    @pl.when(me < peers // 2)
    def _():
        enter()
        send_last()


    loads["cells"].wait()
    rows[0:64] = dot3((edge_cells[0, 0:64], edge_cells[1, 0:64]), a4, NT) + first[0:64]
    forward += [
        copy(2, rows.at[0:32], got_m, {"genome": after[0]}),
        copy(3, rows.at[32:48], got_2, {"genome": after[1]}),
        copy(4, rows.at[48:56], got_3, {"genome": after[2]}),
    ]
    for c in forward[1:]:
        c.start()
    for name in ("table_e", "wide", "prior", "levels", "dead", "direct"):
        load(name, *later[name])
    rows[64:176] = dot3((edge_cells[0, 64:176], edge_cells[1, 64:176]), a4, NT) + first[64:176]
    backward = [
        copy(6, rows.at[72:96], back_1, {"genome": before[0]}),
        copy(7, rows.at[96:112], back_2, {"genome": before[1]}),
        copy(8, rows.at[96:104], back_3, {"genome": before[2]}),
    ]
    near_copy = copy(12, rows.at[120:168], near, {"genome": before[0]})

    def send_backward():
        for i, c in enumerate(backward):
            pl.semaphore_wait(present.at[i], 1)
            c.start()

    pl.when(me > 0)(send_backward)

    for b in range(blocks):
        span = slice(b * BLOCK, (b + 1) * BLOCK)
        p = dot(design, xe[:samples, span], NN)
        high = p.astype(BF16).astype(F32)
        xe[samples:, span] = jnp.concatenate([high, p - high], 0).astype(BF16)

    gram_copy.wait()
    for name in ("prior", "levels", "dead"):
        loads[name].wait()
    lanes = lax.broadcasted_iota(jnp.int32, (8, 128), 1)
    subs = lax.broadcasted_iota(jnp.int32, (8, 128), 0)
    aug = gram_mine[...] + gram_theirs[...] + jnp.where(lanes == subs + 8, 1.0, 0.0)
    for k in range(DESIGN):
        row = aug[k : k + 1, :] / aug[k : k + 1, k : k + 1]
        aug = jnp.where(subs == k, row, aug - aug[:, k : k + 1] * row)
    diagonal = jnp.sum(jnp.where(lanes == subs + 8, aug, 0.0), 1, keepdims=True)
    inverse = [aug[:, 8 + k : 9 + k] for k in range(DESIGN)]
    weights = jnp.zeros(levels.shape, F32)
    for number in range(LEVELS + 1):
        weights = jnp.where(levels[...] == number, prior[number], weights)
    edge_weights = weights[:, BLOCK + 128 :]

    def shrink(m, s, weight):
        effects = inverse[0] * m[0:1]
        for k in range(1, DESIGN):
            effects = effects + inverse[k] * m[k : k + 1]
        left = jnp.sum(s, 0, keepdims=True) - jnp.sum(m * effects, 0, keepdims=True)
        noise = jnp.maximum(left, 0.0) / (total - DESIGN) + 1e-06
        squared = effects * effects
        return squared * effects / (squared + (noise * weight) * diagonal)

    def paired(shrunk):
        high = shrunk.astype(BF16).astype(F32)
        return jnp.concatenate([high, shrunk - high], 0).astype(BF16)

    def both(a, table, dims):
        return dot(a, table[0], dims) + dot(a, table[1], dims)

    def folded(res):
        return res[:8] + res[8:]

    def pick(a):
        return jnp.where(side == 0, a[:4], a[4:])

    only = jnp.where(lax.broadcasted_iota(jnp.int32, (8, 128), 0) == 0, 1.0, 0.0)
    only = only.astype(BF16)

    def summed(u, ref, skip=0):
        blank = [jnp.zeros((n, samples), F32) for n in (skip, 128 - skip - u.shape[0])]
        u = jnp.concatenate([*blank[:1], u, blank[1]] if skip else [u, blank[1]], 0)
        uh, ul = halves(u)
        squares = u * u
        sh, sl = halves(sum(squares[:, i : i + 128] for i in range(0, samples, 128)))
        ref[0:8] = dot(design, uh, NT) + dot(design, ul, NT)
        ref[8:16] = dot(only, sh, NT) + dot(only, sl, NT)

    def shrunk_edge(mine, theirs):
        total_edge = mine[...] + theirs[...]
        return shrink(total_edge[0:8], total_edge[8:16], edge_weights)

    a_copy = copy(9, a_mine, a_theirs, {"sample": 1 - side})
    b_copy = copy(10, b_mine, b_theirs, {"sample": 1 - side})
    su_copy = copy(11, su_ref, su_got, {"genome": before[0]})
    w_copy = copy(13, w_mine, w_theirs, {"sample": 1 - side})

    def u_before():
        return jnp.concatenate([rows[120:152] + got_e[...], rows[152:168] + got_m[0:16]], 0)

    def sum_before():
        forward[0].wait()
        forward[1].wait()
        summed(u_before(), a_mine)
        a_copy.start()

    def shrink_before():
        a_copy.wait()
        su_ref[...] = shrunk_edge(a_mine, a_theirs)

    def give_back():
        shrink_before()
        su_copy.start()

    pl.when(me == 1)(sum_before)
    for name in ("table_e", "wide"):
        loads[name].wait()
    spill = jnp.concatenate([wide[0, BLOCK:, 128:], wide[1, BLOCK:, 128:]], 1)
    e = dot3(a4, (table_e[0], table_e[1]), NN)
    eh, el = halves(e)
    stats_mine[0:8, width - 128 : width] = dot(design, eh, NN) + dot(design, el, NN)
    stats_mine[8:16, width - 128 : width] = jnp.sum((e * e).reshape(samples // 8, 8, 128), 0)
    for b in range(blocks):
        if b == 2:
            pl.when(me == 1)(give_back)
        depth = BLOCK + 128 if b < blocks - 1 else BLOCK
        span = slice(b * BLOCK, (b + 1) * BLOCK)
        window = xe[:, span]
        res = dot(window, wide[0, :BLOCK], NN) + dot(window, wide[1, :BLOCK], NN)
        if depth > BLOCK:
            tail = dot(xe[:, (b + 1) * BLOCK : b * BLOCK + depth], spill, NN)
            res = jnp.concatenate([res[:, :128], res[:, 128:] + tail[:, :128] + tail[:, 128:]], 1)
        main = res[:samples]
        stats_mine[0:8, span] = res[samples : samples + 8] + res[samples + 8 :]
        stats_mine[8:16, span] = jnp.sum((main * main).reshape(samples // 8, 8, BLOCK), 0)
    stats_copy = copy(5, stats_mine, stats_theirs, {"sample": 1 - side})
    stats_copy.start()

    pl.when(me > 1)(sum_before)

    @pl.when(me == 0)
    def _():
        send_backward()
        near_copy.start()


    stats_copy.wait()
    lane = lax.broadcasted_iota(jnp.int32, (8, BLOCK), 1)
    coarse = (lane >= 128) & (lane < 144)
    for b in range(blocks):
        span = slice(b * BLOCK, (b + 1) * BLOCK)
        m = stats_mine[0:8, span] + stats_theirs[0:8, span]
        s = stats_mine[8:16, span] + stats_theirs[8:16, span]
        g = jnp.where(coarse, 0.0, shrink(m, s, weights[:, :BLOCK]))
        if b == blocks - 1:
            g = jnp.where(dead[...] > 0, 0.0, g)
        stack[16 * b : 16 * b + 16, :] = paired(g)
    span = slice(width - 128, width)
    m = stats_mine[0:8, span] + stats_theirs[0:8, span]
    s = stats_mine[8:16, span] + stats_theirs[8:16, span]
    se = paired(shrink(m, s, weights[:, BLOCK : BLOCK + 128]))
    pl.when(me > 1)(give_back)

    y_main[...] = both(stack[...], (wide[0], wide[1]), NT)
    a4_main[...] = both(se, (table_e[0], table_e[1]), NT)

    a4 = folded(a4_main[...])
    narrow = lax.broadcasted_iota(jnp.int32, (8, 128), 1) < 16
    for b in range(blocks):
        moved = a4 if b == 0 else pltpu.roll(a4, 128 - 16 * b, 1)
        stack[16 * b : 16 * b + 16, :128] = paired(jnp.where(narrow, moved, 0.0))
    y = y_main[...] + both(stack[:, :128], (wide[0, :, 128:256], wide[1, :, 128:256]), NT)
    begin = jnp.zeros((8, 128), F32)
    for b in range(blocks):
        piece = folded(y[16 * b : 16 * b + 16])
        y_ref[:, b * BLOCK : b * BLOCK + 128] = pick(piece[:, :128] + begin)
        y_ref[:, b * BLOCK + 128 : (b + 1) * BLOCK] = pick(piece[:, 128:256])
        begin = piece[:, 256:]


    for c in backward + forward[2:]:
        c.wait()

    def u_long():
        u = rows[56:72] + got_m[16:32] + got_2[...] + back_1[0:16]
        return jnp.concatenate(
            [
                u[0:8] + back_2[0:8],
                u[8:16] + got_3[...],
                rows[112:120] + back_1[16:24] + back_2[8:16] + back_3[...],
            ],
            0,
        )

    @pl.when(me == 0)
    def _():
        forward[0].wait()
        forward[1].wait()
        summed(jnp.concatenate([u_before(), u_long()], 0), b_mine)
        su_ref[...] = jnp.zeros(su_ref.shape, F32)

    @pl.when(me > 0)
    def _():
        summed(u_long(), b_mine, 48)

    b_copy.start()

    @pl.when(me == peers - 1)
    def _():
        near_copy.wait_recv()
        summed(jnp.concatenate([own_e[...] + near[0:32], rows[0:16] + near[32:48]], 0), w_mine)
        w_copy.start()
        w_copy.wait()
        su_got[...] = shrunk_edge(w_mine, w_theirs)

    loads["direct"].wait()
    b_copy.wait()
    b_shrunk = shrunk_edge(b_mine, b_theirs)
    pl.when(me < peers - 1)(su_copy.wait_recv)
    su = pick(su_ref[...] + b_shrunk + pltpu.roll(su_got[...], 80, 1))
    last = both(paired(su), (direct[0], direct[1]), NN)
    out[...] = y_ref[...] + last[:4] + last[4:]
    pl.when(me > 0)(su_copy.wait_send)
    pl.when(me == 0)(near_copy.wait_send)


def local(signal, coverage, design_codes, level_prior):
    samples, length = signal.shape
    blocks = length // BLOCK
    *pairs, l_main, l_e, l_u, straddles = tables(length)
    pieces = [jnp.asarray(two(t)) for t in pairs]
    levels = jnp.asarray(np.concatenate([l_main, l_e, l_u])[None])
    dead = jnp.asarray(straddles.astype(np.int32)[None])
    total = samples * lax.axis_size("sample")
    width = blocks * BLOCK + 128
    operands = (signal, coverage, design_codes, level_prior, levels, dead, *pieces)
    places = [pltpu.VMEM(a.shape, a.dtype) for a in operands]
    places[3] = pltpu.SMEM(level_prior.shape, F32)
    copies = 14
    return pl.pallas_call(
        functools.partial(kernel, total),
        out_shape=pltpu.VMEM((DESIGN // lax.axis_size("sample"), length), F32),
        in_specs=[pl.BlockSpec(memory_space=pltpu.HBM)] * len(operands),
        out_specs=pl.BlockSpec(memory_space=pltpu.VMEM),
        scratch_shapes=places
        + [
            pltpu.VMEM((8, samples), F32),
            pltpu.VMEM((samples + 16, length), BF16),
            pltpu.VMEM((length, 256), BF16),
            pltpu.VMEM((32, samples), F32),
            pltpu.VMEM((176, samples), F32),
            pltpu.VMEM((32, samples), F32),
            pltpu.VMEM((32, samples), F32),
            pltpu.VMEM((16, samples), F32),
            pltpu.VMEM((8, samples), F32),
            pltpu.VMEM((24, samples), F32),
            pltpu.VMEM((16, samples), F32),
            pltpu.VMEM((8, samples), F32),
            pltpu.VMEM((8, 128), F32),
            pltpu.VMEM((8, 128), F32),
            pltpu.VMEM((16, width), F32),
            pltpu.VMEM((16, width), F32),
            pltpu.VMEM((48, samples), F32),
            pltpu.VMEM((16, 128), F32),
            pltpu.VMEM((16, 128), F32),
            pltpu.VMEM((16, 128), F32),
            pltpu.VMEM((16, 128), F32),
            pltpu.VMEM((16, 128), F32),
            pltpu.VMEM((16, 128), F32),
            pltpu.VMEM((8, 128), F32),
            pltpu.VMEM((8, 128), F32),
            pltpu.VMEM((16 * blocks, BLOCK), BF16),
            pltpu.VMEM((4, length), F32),
            pltpu.VMEM((16 * blocks, BLOCK + 128), F32),
            pltpu.VMEM((16, 128), F32),
            pltpu.SemaphoreType.DMA((11 + 2 * (length // CHUNK),)),
            pltpu.SemaphoreType.DMA((copies,)),
            pltpu.SemaphoreType.DMA((copies,)),
            pltpu.SemaphoreType.REGULAR((3,)),
        ],
        compiler_params=pltpu.CompilerParams(
            collective_id=0, has_side_effects=True, vmem_limit_bytes=56 * 2**20
        ),
    )(*operands)


def solution(mesh):
    placed = (
        P("sample", ("parts", "genome")),
        P("sample", ("parts", "genome")),
        P(None, "sample"),
        P(),
    )
    return jax.shard_map(
        local,
        mesh=mesh,
        in_specs=placed,
        out_specs=P("sample", ("parts", "genome")),
        check_vma=False,
    )
```

```python
import functools

import jax
import jax.numpy as jnp
import ml_dtypes
import numpy as np
from jax import lax
from jax.experimental import pallas as pl
from jax.experimental.pallas import tpu as pltpu
from jax.sharding import PartitionSpec as P

LEVELS = 10
DESIGN = 8
FINE = 4
BLOCK = 256
TAIL = 512
LOWPASS = np.array(
    (
        0.23037781330885523,
        0.7148465705525415,
        0.6308807679295904,
        -0.02798376941698385,
        -0.18703481171888114,
        0.030841381835986965,
        0.032883011666982945,
        -0.010597401784997278,
    )
)
HIGHPASS = np.array([(-1.0) ** m * LOWPASS[7 - m] for m in range(8)])


def spread(taps, step):
    out = np.zeros(7 * step + 1)
    out[::step] = taps
    return out


def composite(levels):
    low = np.ones(1)
    details = []
    for j in range(levels):
        details.append(np.convolve(low, spread(HIGHPASS, 2**j)))
        low = np.convolve(low, spread(LOWPASS, 2**j))
    return details, low


def column(taps, start, size):
    out = np.zeros(size)
    for i, tap in enumerate(taps):
        if 0 <= start + i < size:
            out[start + i] = tap
    return out


def tables(length):
    det, low = composite(LEVELS)
    fine_low = composite(FINE)[1]
    coarse_det, coarse_low = composite(LEVELS - FINE)
    cells = length >> FINE
    group1 = [(1, k) for k in range(125)] + [(2, k) for k in range(3)]
    group2 = [(0, k) for k in range(16)] + [(4, k) for k in range(16)] + [(3, k) for k in range(32)]
    group2 += [(2, k) for k in range(3, 64)] + [(1, k) for k in range(125, 128)]
    wide = np.zeros((BLOCK + 128, 2 * 128))
    level_main = np.zeros(256, np.int32)
    straddles = np.zeros(256, bool)
    for c, (level, k) in enumerate(group1 + group2):
        taps = det[level - 1] if level else fine_low
        step = 2 ** (level or FINE)
        wide[:, c] = column(taps, step * k, BLOCK + 128)
        level_main[c] = (level or 1) - 1
        straddles[c] = level > 0 and step * k + len(taps) > BLOCK
    coarse = [(level, k) for level in range(FINE + 1, LEVELS + 1) for k in range(length >> level)]
    coarse += [(0, k) for k in range(length >> LEVELS)]
    table_e = np.zeros((cells, 128))
    level_e = np.zeros(128, np.int32)
    for c, (level, k) in enumerate(coarse):
        taps = coarse_det[level - FINE - 1] if level else coarse_low
        step = 2 ** ((level or LEVELS) - FINE)
        level_e[c] = level - 1 if level else LEVELS
        full = det[level - 1] if level else low
        if (step << FINE) * k + len(full) <= length:
            table_e[:, c] = column(taps, step * k, cells)
    edge = []
    for level in range(1, LEVELS + 1):
        size = length >> level
        first = -(-(length - len(det[level - 1]) + 1) // 2**level)
        edge += [(level, k) for k in range(max(first, 0), size)]
    early = [e for e in edge if e[0] < 7]
    middle = [e for e in edge if 7 <= e[0] < 9 or (e[0] == 9 and e[1] < 2)]
    late = [e for e in edge if e not in early + middle] + [(0, k) for k in range(length >> LEVELS)]
    early += [None] * (32 - len(early))
    middle += [None] * (16 - len(middle))
    late += [None] * (8 - len(late))
    coarsest = late[2:6]
    none = [None] * 2
    sets = [row for row in late if row]
    levels = np.zeros(128, np.int32)
    for r, row in enumerate(early + middle + sets + sets + coarsest + late):
        if row:
            levels[r] = row[0] - 1 if row[0] else LEVELS
    shifted = []
    for shift, part in (
        (0, middle + sets), (1, sets), (2, coarsest),
        (0, 3 * none + sets), (1, coarsest),
        (0, 2 * none + coarsest),
        (1, sets), (2, sets), (3, coarsest),
        (2, sets), (3, sets), (0, 2 * none), (1, late),
        (3, late), (2, late),
        (0, late),
        (1, early + middle),
    ):
        shifted += [(row, shift * length) for row in part]
    edge_cells = np.zeros((176, cells))
    edge_first = np.zeros((176, 128))
    edge_last = np.zeros((32, TAIL))
    direct = np.zeros((128, length))
    into = {**{120 + r: r for r in range(48)}, **{56 + r: 48 + r for r in range(16)}, **{112 + r: 64 + r for r in range(8)}}
    for r, (row, shift) in enumerate(shifted):
        if row is None:
            continue
        level, k = row
        if r in into:
            full = det[level - 1] if level else low
            direct[into[r]] = column(full, k * 2 ** (level or LEVELS) - shift, length)
        if 1 <= level <= FINE:
            edge_first[r] = column(det[level - 1], k * 2**level - shift, 128)
            continue
        taps = coarse_det[level - FINE - 1] if level else coarse_low
        start = k * 2 ** ((level or LEVELS) - FINE) - (shift >> FINE)
        edge_cells[r] = column(taps, start, cells)
        for c in range(-6, 0):
            if 0 <= c - start < len(taps):
                edge_first[r] += taps[c - start] * column(fine_low, c * 2**FINE, 128)
    for r, row in enumerate(early + middle):
        if row:
            direct[80 + r] = column(det[row[0] - 1], row[1] * 2 ** row[0], length)
    for r, row in enumerate(early):
        if row:
            edge_last[r] = column(det[row[0] - 1], row[1] * 2 ** row[0] - (length - TAIL), TAIL)
    base = np.stack([column(fine_low, (k if k < 16 else k - 128) * 2**FINE, BLOCK) for k in range(128)], 1)
    return base, wide, table_e, edge_cells, edge_first, edge_last, direct, level_main, level_e, levels, straddles


def two(table):
    high = table.astype(np.float32).astype(ml_dtypes.bfloat16)
    rest = (table - high.astype(np.float64)).astype(np.float32).astype(ml_dtypes.bfloat16)
    return np.stack([high, rest])


NN = (((1,), (0,)), ((), ()))
NT = (((1,), (1,)), ((), ()))


def dot(a, b, dims):
    return lax.dot_general(a, b, dims, preferred_element_type=jnp.float32)


def halves(a):
    high = a.astype(jnp.bfloat16)
    return high, (a - high.astype(jnp.float32)).astype(jnp.bfloat16)


def dot3(a, b, dims):
    return dot(a[0], b[0], dims) + dot(a[0], b[1], dims) + dot(a[1], b[0], dims)


CHUNK = 512
F32 = jnp.float32
BF16 = jnp.bfloat16


def kernel(total, *refs):
    inputs = refs[:13]
    out = refs[13]
    loaded = refs[14:27]
    (
        d_ref,
        xe,
        dense,
        own_e,
        rows,
        got_e,
        got_m,
        got_2,
        got_3,
        back_1,
        back_2,
        back_3,
        gram_mine,
        gram_theirs,
        stats_mine,
        stats_theirs,
        near,
        a_mine,
        a_theirs,
        b_mine,
        b_theirs,
        w_mine,
        w_theirs,
        su_ref,
        su_got,
        stack,
        y_ref,
        y_main,
        a4_main,
        load_sem,
        send_sem,
        recv_sem,
        present,
    ) = refs[27:]
    signal, coverage = loaded[:2]
    codes, prior, levels, dead, base, wide, table_e, edge_cells, edge_first, edge_last, direct = loaded[2:]
    samples, length = signal.shape
    blocks = length // BLOCK
    chunks = length // CHUNK
    width = blocks * BLOCK + 128
    me = lax.axis_index("genome")
    peers = lax.axis_size("genome")
    side = lax.axis_index("sample")
    before = [lax.rem(me + peers - i, peers) for i in (1, 2, 3)]
    after = [lax.rem(me + i, peers) for i in (1, 2, 3)]

    barrier = pltpu.get_barrier_semaphore()
    for peer in before:
        pl.semaphore_signal(barrier, inc=1, device_id={"genome": peer})
    pl.semaphore_signal(barrier, inc=1, device_id={"sample": 1 - side})

    loads = {}

    def load(name, src, dst):
        c = pltpu.make_async_copy(src, dst, load_sem.at[len(loads)])
        c.start()
        loads[name] = c

    def load_chunk(i):
        span = pl.ds(i * CHUNK, CHUNK)
        load(("signal", i), inputs[0].at[:, span], signal.at[:, span])
        load(("coverage", i), inputs[1].at[:, span], coverage.at[:, span])

    names = ("codes", "prior", "levels", "dead", "base", "wide", "table_e", "cells", "first", "last", "direct")
    later = dict(zip(names, zip(inputs[2:], loaded[2:])))
    order = [chunks - 1, *range(chunks - 1)]
    load("base", *later["base"])
    load("codes", *later["codes"])
    load_chunk(order[0])
    load("last", *later["last"])
    load_chunk(order[1])
    load("first", *later["first"])
    for i in order[2:]:
        load_chunk(i)
    load("cells", *later["cells"])

    def copy(number, src, dst, device):
        return pltpu.make_async_remote_copy(
            src_ref=src,
            dst_ref=dst,
            send_sem=send_sem.at[number],
            recv_sem=recv_sem.at[number],
            device_id=device,
            device_id_type=pl.DeviceIdType.MESH,
        )

    loads["codes"].wait()
    d_ref[0:1, :] = jnp.ones((1, samples), F32)
    d_ref[1:8, :] = codes[...].astype(F32) - 2.0
    design = d_ref[...].astype(BF16)
    padded = jnp.concatenate([d_ref[...], jnp.zeros((120, samples), F32)], 0)
    gram_mine[...] = dot(design, padded.astype(BF16), NT)
    loads["base"].wait()
    for half in range(2):
        part = base[half].astype(F32)
        lane = lax.broadcasted_iota(jnp.int32, part.shape, 1)
        for b in range(blocks):
            moved = jnp.where(lane < 16, part, 0.0) if b == 0 else pltpu.roll(part, 16 * b, 1)
            dense[b * BLOCK : (b + 1) * BLOCK, half * 128 : half * 128 + 128] = moved.astype(BF16)

    def enter():
        pl.semaphore_wait(barrier, 4)
        for i, peer in enumerate(after):
            pl.semaphore_signal(present.at[i], inc=1, device_id={"genome": peer})

    def send_last():
        forward[0].start()
        gram_copy.start()

    forward = [copy(0, own_e, got_e, {"genome": after[0]})]
    gram_copy = copy(1, gram_mine, gram_theirs, {"sample": 1 - side})
    pl.when(me >= peers // 2)(enter)
    a4 = None
    for i in order:
        loads["signal", i].wait()
        loads["coverage", i].wait()
        span = slice(i * CHUNK, (i + 1) * CHUNK)
        x = (signal[:, span].astype(F32) * coverage[:, span].astype(F32)).astype(BF16)
        xe[:samples, span] = x
        if i == chunks - 1:
            loads["last"].wait()
            pair = dot(edge_last[...].reshape(64, TAIL), x, NT)
            own_e[...] = pair[:32] + pair[32:]
            pl.when(me >= peers // 2)(send_last)
        if i == 0:
            loads["first"].wait()
            pair = dot(edge_first[...].reshape(352, 128), x[:, :128], NT)
            first = pair[:176] + pair[176:]
        piece = dot(x, dense[span], NN)
        a4 = piece if a4 is None else a4 + piece
    a4 = halves(a4[:, :128] + a4[:, 128:])

    @pl.when(me < peers // 2)
    def _():
        enter()
        send_last()


    loads["cells"].wait()
    rows[0:64] = dot3((edge_cells[0, 0:64], edge_cells[1, 0:64]), a4, NT) + first[0:64]
    forward += [
        copy(2, rows.at[0:32], got_m, {"genome": after[0]}),
        copy(3, rows.at[32:48], got_2, {"genome": after[1]}),
        copy(4, rows.at[48:56], got_3, {"genome": after[2]}),
    ]
    for c in forward[1:]:
        c.start()
    for name in ("table_e", "wide", "prior", "levels", "dead", "direct"):
        load(name, *later[name])
    rows[64:176] = dot3((edge_cells[0, 64:176], edge_cells[1, 64:176]), a4, NT) + first[64:176]
    backward = [
        copy(6, rows.at[72:96], back_1, {"genome": before[0]}),
        copy(7, rows.at[96:112], back_2, {"genome": before[1]}),
        copy(8, rows.at[96:104], back_3, {"genome": before[2]}),
    ]
    near_copy = copy(12, rows.at[120:168], near, {"genome": before[0]})

    def send_backward():
        for i, c in enumerate(backward):
            pl.semaphore_wait(present.at[i], 1)
            c.start()

    pl.when(me > 0)(send_backward)

    for b in range(blocks):
        span = slice(b * BLOCK, (b + 1) * BLOCK)
        p = dot(design, xe[:samples, span], NN)
        high = p.astype(BF16).astype(F32)
        xe[samples:, span] = jnp.concatenate([high, p - high], 0).astype(BF16)

    gram_copy.wait()
    for name in ("prior", "levels", "dead"):
        loads[name].wait()
    lanes = lax.broadcasted_iota(jnp.int32, (8, 128), 1)
    subs = lax.broadcasted_iota(jnp.int32, (8, 128), 0)
    aug = gram_mine[...] + gram_theirs[...] + jnp.where(lanes == subs + 8, 1.0, 0.0)
    for k in range(DESIGN):
        row = aug[k : k + 1, :] / aug[k : k + 1, k : k + 1]
        aug = jnp.where(subs == k, row, aug - aug[:, k : k + 1] * row)
    diagonal = jnp.sum(jnp.where(lanes == subs + 8, aug, 0.0), 1, keepdims=True)
    inverse = [aug[:, 8 + k : 9 + k] for k in range(DESIGN)]
    weights = jnp.zeros(levels.shape, F32)
    for number in range(LEVELS + 1):
        weights = jnp.where(levels[...] == number, prior[number], weights)
    edge_weights = weights[:, BLOCK + 128 :]

    def shrink(m, s, weight):
        effects = inverse[0] * m[0:1]
        for k in range(1, DESIGN):
            effects = effects + inverse[k] * m[k : k + 1]
        left = jnp.sum(s, 0, keepdims=True) - jnp.sum(m * effects, 0, keepdims=True)
        noise = jnp.maximum(left, 0.0) / (total - DESIGN) + 1e-06
        squared = effects * effects
        return squared * effects / (squared + (noise * weight) * diagonal)

    def paired(shrunk):
        high = shrunk.astype(BF16).astype(F32)
        return jnp.concatenate([high, shrunk - high], 0).astype(BF16)

    def both(a, table, dims):
        return dot(a, table[0], dims) + dot(a, table[1], dims)

    def folded(res):
        return res[:8] + res[8:]

    def pick(a):
        return jnp.where(side == 0, a[:4], a[4:])

    only = jnp.where(lax.broadcasted_iota(jnp.int32, (8, 128), 0) == 0, 1.0, 0.0)
    only = only.astype(BF16)

    design2 = jnp.concatenate([design, design], 1)
    only2 = jnp.concatenate([only, only], 1)

    def summed(u, ref, skip=0):
        blank = [jnp.zeros((n, samples), F32) for n in (skip, 128 - skip - u.shape[0])]
        u = jnp.concatenate([*blank[:1], u, blank[1]] if skip else [u, blank[1]], 0)
        uh, ul = halves(u)
        squares = u * u
        sh, sl = halves(sum(squares[:, i : i + 128] for i in range(0, samples, 128)))
        ref[0:8] = dot(design2, jnp.concatenate([uh, ul], 1), NT)
        ref[8:16] = dot(only2, jnp.concatenate([sh, sl], 1), NT)

    def shrunk_edge(mine, theirs):
        total_edge = mine[...] + theirs[...]
        return shrink(total_edge[0:8], total_edge[8:16], edge_weights)

    a_copy = copy(9, a_mine, a_theirs, {"sample": 1 - side})
    b_copy = copy(10, b_mine, b_theirs, {"sample": 1 - side})
    su_copy = copy(11, su_ref, su_got, {"genome": before[0]})
    w_copy = copy(13, w_mine, w_theirs, {"sample": 1 - side})

    def u_before():
        return jnp.concatenate([rows[120:152] + got_e[...], rows[152:168] + got_m[0:16]], 0)

    def sum_before():
        forward[0].wait()
        forward[1].wait()
        summed(u_before(), a_mine)
        a_copy.start()

    def shrink_before():
        a_copy.wait()
        su_ref[...] = shrunk_edge(a_mine, a_theirs)

    def give_back():
        shrink_before()
        su_copy.start()

    pl.when(me == 1)(sum_before)
    for name in ("table_e", "wide"):
        loads[name].wait()
    spill = jnp.concatenate([wide[0, BLOCK:, 128:], wide[1, BLOCK:, 128:]], 1)
    e = dot3(a4, (table_e[0], table_e[1]), NN)
    eh, el = halves(e)
    stats_mine[0:8, width - 128 : width] = dot(design, eh, NN) + dot(design, el, NN)
    stats_mine[8:16, width - 128 : width] = jnp.sum((e * e).reshape(samples // 8, 8, 128), 0)
    for b in range(blocks):
        if b == 2:
            pl.when(me == 1)(give_back)
        depth = BLOCK + 128 if b < blocks - 1 else BLOCK
        span = slice(b * BLOCK, (b + 1) * BLOCK)
        window = xe[:, span]
        res = dot(window, wide[0, :BLOCK], NN) + dot(window, wide[1, :BLOCK], NN)
        if depth > BLOCK:
            tail = dot(xe[:, (b + 1) * BLOCK : b * BLOCK + depth], spill, NN)
            res = jnp.concatenate([res[:, :128], res[:, 128:] + tail[:, :128] + tail[:, 128:]], 1)
        main = res[:samples]
        stats_mine[0:8, span] = res[samples : samples + 8] + res[samples + 8 :]
        stats_mine[8:16, span] = jnp.sum((main * main).reshape(samples // 8, 8, BLOCK), 0)
    stats_copy = copy(5, stats_mine, stats_theirs, {"sample": 1 - side})
    stats_copy.start()

    pl.when(me > 1)(sum_before)

    @pl.when(me == 0)
    def _():
        send_backward()
        near_copy.start()


    stats_copy.wait()
    lane = lax.broadcasted_iota(jnp.int32, (8, BLOCK), 1)
    coarse = (lane >= 128) & (lane < 144)
    for b in range(blocks):
        span = slice(b * BLOCK, (b + 1) * BLOCK)
        m = stats_mine[0:8, span] + stats_theirs[0:8, span]
        s = stats_mine[8:16, span] + stats_theirs[8:16, span]
        g = jnp.where(coarse, 0.0, shrink(m, s, weights[:, :BLOCK]))
        if b == blocks - 1:
            g = jnp.where(dead[...] > 0, 0.0, g)
        stack[16 * b : 16 * b + 16, :] = paired(g)
    span = slice(width - 128, width)
    m = stats_mine[0:8, span] + stats_theirs[0:8, span]
    s = stats_mine[8:16, span] + stats_theirs[8:16, span]
    se = paired(shrink(m, s, weights[:, BLOCK : BLOCK + 128]))
    pl.when(me > 1)(give_back)

    y_main[...] = both(stack[...], (wide[0], wide[1]), NT)
    a4_main[...] = both(se, (table_e[0], table_e[1]), NT)

    a4 = folded(a4_main[...])
    narrow = lax.broadcasted_iota(jnp.int32, (8, 128), 1) < 16
    for b in range(blocks):
        moved = a4 if b == 0 else pltpu.roll(a4, 128 - 16 * b, 1)
        stack[16 * b : 16 * b + 16, :128] = paired(jnp.where(narrow, moved, 0.0))
    y = y_main[...] + both(stack[:, :128], (wide[0, :, 128:256], wide[1, :, 128:256]), NT)
    begin = jnp.zeros((8, 128), F32)
    for b in range(blocks):
        piece = folded(y[16 * b : 16 * b + 16])
        y_ref[:, b * BLOCK : b * BLOCK + 128] = pick(piece[:, :128] + begin)
        y_ref[:, b * BLOCK + 128 : (b + 1) * BLOCK] = pick(piece[:, 128:256])
        begin = piece[:, 256:]


    for c in backward + forward[2:]:
        c.wait()

    def u_long():
        u = rows[56:72] + got_m[16:32] + got_2[...] + back_1[0:16]
        return jnp.concatenate(
            [
                u[0:8] + back_2[0:8],
                u[8:16] + got_3[...],
                rows[112:120] + back_1[16:24] + back_2[8:16] + back_3[...],
            ],
            0,
        )

    @pl.when(me == 0)
    def _():
        forward[0].wait()
        forward[1].wait()
        summed(jnp.concatenate([u_before(), u_long()], 0), b_mine)
        su_ref[...] = jnp.zeros(su_ref.shape, F32)

    @pl.when(me > 0)
    def _():
        summed(u_long(), b_mine, 48)

    b_copy.start()

    @pl.when(me == peers - 1)
    def _():
        near_copy.wait_recv()
        summed(jnp.concatenate([own_e[...] + near[0:32], rows[0:16] + near[32:48]], 0), w_mine)
        w_copy.start()
        w_copy.wait()
        su_got[...] = shrunk_edge(w_mine, w_theirs)

    loads["direct"].wait()
    b_copy.wait()
    b_shrunk = shrunk_edge(b_mine, b_theirs)
    pl.when(me < peers - 1)(su_copy.wait_recv)
    su = pick(su_ref[...] + b_shrunk + pltpu.roll(su_got[...], 80, 1))
    last = both(paired(su), (direct[0], direct[1]), NN)
    out[...] = y_ref[...] + last[:4] + last[4:]
    pl.when(me > 0)(su_copy.wait_send)
    pl.when(me == 0)(near_copy.wait_send)


def local(signal, coverage, design_codes, level_prior):
    samples, length = signal.shape
    blocks = length // BLOCK
    *pairs, l_main, l_e, l_u, straddles = tables(length)
    pieces = [jnp.asarray(two(t)) for t in pairs]
    levels = jnp.asarray(np.concatenate([l_main, l_e, l_u])[None])
    dead = jnp.asarray(straddles.astype(np.int32)[None])
    total = samples * lax.axis_size("sample")
    width = blocks * BLOCK + 128
    operands = (signal, coverage, design_codes, level_prior, levels, dead, *pieces)
    places = [pltpu.VMEM(a.shape, a.dtype) for a in operands]
    places[3] = pltpu.SMEM(level_prior.shape, F32)
    copies = 14
    return pl.pallas_call(
        functools.partial(kernel, total),
        out_shape=pltpu.VMEM((DESIGN // lax.axis_size("sample"), length), F32),
        in_specs=[pl.BlockSpec(memory_space=pltpu.HBM)] * len(operands),
        out_specs=pl.BlockSpec(memory_space=pltpu.VMEM),
        scratch_shapes=places
        + [
            pltpu.VMEM((8, samples), F32),
            pltpu.VMEM((samples + 16, length), BF16),
            pltpu.VMEM((length, 256), BF16),
            pltpu.VMEM((32, samples), F32),
            pltpu.VMEM((176, samples), F32),
            pltpu.VMEM((32, samples), F32),
            pltpu.VMEM((32, samples), F32),
            pltpu.VMEM((16, samples), F32),
            pltpu.VMEM((8, samples), F32),
            pltpu.VMEM((24, samples), F32),
            pltpu.VMEM((16, samples), F32),
            pltpu.VMEM((8, samples), F32),
            pltpu.VMEM((8, 128), F32),
            pltpu.VMEM((8, 128), F32),
            pltpu.VMEM((16, width), F32),
            pltpu.VMEM((16, width), F32),
            pltpu.VMEM((48, samples), F32),
            pltpu.VMEM((16, 128), F32),
            pltpu.VMEM((16, 128), F32),
            pltpu.VMEM((16, 128), F32),
            pltpu.VMEM((16, 128), F32),
            pltpu.VMEM((16, 128), F32),
            pltpu.VMEM((16, 128), F32),
            pltpu.VMEM((8, 128), F32),
            pltpu.VMEM((8, 128), F32),
            pltpu.VMEM((16 * blocks, BLOCK), BF16),
            pltpu.VMEM((4, length), F32),
            pltpu.VMEM((16 * blocks, BLOCK + 128), F32),
            pltpu.VMEM((16, 128), F32),
            pltpu.SemaphoreType.DMA((11 + 2 * (length // CHUNK),)),
            pltpu.SemaphoreType.DMA((copies,)),
            pltpu.SemaphoreType.DMA((copies,)),
            pltpu.SemaphoreType.REGULAR((3,)),
        ],
        compiler_params=pltpu.CompilerParams(
            collective_id=0, has_side_effects=True, vmem_limit_bytes=56 * 2**20
        ),
    )(*operands)


def solution(mesh):
    placed = (
        P("sample", ("parts", "genome")),
        P("sample", ("parts", "genome")),
        P(None, "sample"),
        P(),
    )
    return jax.shard_map(
        local,
        mesh=mesh,
        in_specs=placed,
        out_specs=P("sample", ("parts", "genome")),
        check_vma=False,
    )
```

```python
import functools

import jax
import jax.numpy as jnp
import ml_dtypes
import numpy as np
from jax import lax
from jax.experimental import pallas as pl
from jax.experimental.pallas import tpu as pltpu
from jax.sharding import PartitionSpec as P

LEVELS = 10
DESIGN = 8
FINE = 4
BLOCK = 256
TAIL = 512
LOWPASS = np.array(
    (
        0.23037781330885523,
        0.7148465705525415,
        0.6308807679295904,
        -0.02798376941698385,
        -0.18703481171888114,
        0.030841381835986965,
        0.032883011666982945,
        -0.010597401784997278,
    )
)
HIGHPASS = np.array([(-1.0) ** m * LOWPASS[7 - m] for m in range(8)])


def spread(taps, step):
    out = np.zeros(7 * step + 1)
    out[::step] = taps
    return out


def composite(levels):
    low = np.ones(1)
    details = []
    for j in range(levels):
        details.append(np.convolve(low, spread(HIGHPASS, 2**j)))
        low = np.convolve(low, spread(LOWPASS, 2**j))
    return details, low


def column(taps, start, size):
    out = np.zeros(size)
    for i, tap in enumerate(taps):
        if 0 <= start + i < size:
            out[start + i] = tap
    return out


def tables(length):
    det, low = composite(LEVELS)
    fine_low = composite(FINE)[1]
    coarse_det, coarse_low = composite(LEVELS - FINE)
    cells = length >> FINE
    group1 = [(1, k) for k in range(125)] + [(2, k) for k in range(3)]
    group2 = [(0, k) for k in range(16)] + [(4, k) for k in range(16)] + [(3, k) for k in range(32)]
    group2 += [(2, k) for k in range(3, 64)] + [(1, k) for k in range(125, 128)]
    wide = np.zeros((BLOCK + 128, 2 * 128))
    level_main = np.zeros(256, np.int32)
    straddles = np.zeros(256, bool)
    for c, (level, k) in enumerate(group1 + group2):
        taps = det[level - 1] if level else fine_low
        step = 2 ** (level or FINE)
        wide[:, c] = column(taps, step * k, BLOCK + 128)
        level_main[c] = (level or 1) - 1
        straddles[c] = level > 0 and step * k + len(taps) > BLOCK
    coarse = [(level, k) for level in range(FINE + 1, LEVELS + 1) for k in range(length >> level)]
    coarse += [(0, k) for k in range(length >> LEVELS)]
    table_e = np.zeros((cells, 128))
    level_e = np.zeros(128, np.int32)
    for c, (level, k) in enumerate(coarse):
        taps = coarse_det[level - FINE - 1] if level else coarse_low
        step = 2 ** ((level or LEVELS) - FINE)
        level_e[c] = level - 1 if level else LEVELS
        full = det[level - 1] if level else low
        if (step << FINE) * k + len(full) <= length:
            table_e[:, c] = column(taps, step * k, cells)
    edge = []
    for level in range(1, LEVELS + 1):
        size = length >> level
        first = -(-(length - len(det[level - 1]) + 1) // 2**level)
        edge += [(level, k) for k in range(max(first, 0), size)]
    early = [e for e in edge if e[0] < 7]
    middle = [e for e in edge if 7 <= e[0] < 9 or (e[0] == 9 and e[1] < 2)]
    late = [e for e in edge if e not in early + middle] + [(0, k) for k in range(length >> LEVELS)]
    early += [None] * (32 - len(early))
    middle += [None] * (16 - len(middle))
    late += [None] * (8 - len(late))
    coarsest = late[2:6]
    none = [None] * 2
    sets = [row for row in late if row]
    levels = np.zeros(128, np.int32)
    for r, row in enumerate(early + middle + sets + sets + coarsest + late):
        if row:
            levels[r] = row[0] - 1 if row[0] else LEVELS
    shifted = []
    for shift, part in (
        (0, middle + sets), (1, sets), (2, coarsest),
        (0, 3 * none + sets), (1, coarsest),
        (0, 2 * none + coarsest),
        (1, sets), (2, sets), (3, coarsest),
        (2, sets), (3, sets), (0, 2 * none), (1, late),
        (3, late), (2, late),
        (0, late),
        (1, early + middle),
    ):
        shifted += [(row, shift * length) for row in part]
    edge_cells = np.zeros((176, cells))
    edge_first = np.zeros((176, 128))
    edge_last = np.zeros((32, TAIL))
    direct = np.zeros((128, length))
    into = {**{120 + r: r for r in range(48)}, **{56 + r: 48 + r for r in range(16)}, **{112 + r: 64 + r for r in range(8)}}
    for r, (row, shift) in enumerate(shifted):
        if row is None:
            continue
        level, k = row
        if r in into:
            full = det[level - 1] if level else low
            direct[into[r]] = column(full, k * 2 ** (level or LEVELS) - shift, length)
        if 1 <= level <= FINE:
            edge_first[r] = column(det[level - 1], k * 2**level - shift, 128)
            continue
        taps = coarse_det[level - FINE - 1] if level else coarse_low
        start = k * 2 ** ((level or LEVELS) - FINE) - (shift >> FINE)
        edge_cells[r] = column(taps, start, cells)
        for c in range(-6, 0):
            if 0 <= c - start < len(taps):
                edge_first[r] += taps[c - start] * column(fine_low, c * 2**FINE, 128)
    for r, row in enumerate(early + middle):
        if row:
            direct[80 + r] = column(det[row[0] - 1], row[1] * 2 ** row[0], length)
    for r, row in enumerate(early):
        if row:
            edge_last[r] = column(det[row[0] - 1], row[1] * 2 ** row[0] - (length - TAIL), TAIL)
    base = np.stack([column(fine_low, (k if k < 16 else k - 128) * 2**FINE, BLOCK) for k in range(128)], 1)
    return base, wide, table_e, edge_cells, edge_first, edge_last, direct, level_main, level_e, levels, straddles


def two(table):
    high = table.astype(np.float32).astype(ml_dtypes.bfloat16)
    rest = (table - high.astype(np.float64)).astype(np.float32).astype(ml_dtypes.bfloat16)
    return np.stack([high, rest])


NN = (((1,), (0,)), ((), ()))
NT = (((1,), (1,)), ((), ()))


def dot(a, b, dims):
    return lax.dot_general(a, b, dims, preferred_element_type=jnp.float32)


def halves(a):
    high = a.astype(jnp.bfloat16)
    return high, (a - high.astype(jnp.float32)).astype(jnp.bfloat16)


def dot3(a, b, dims):
    return dot(a[0], b[0], dims) + dot(a[0], b[1], dims) + dot(a[1], b[0], dims)


CHUNK = 512
F32 = jnp.float32
BF16 = jnp.bfloat16


def kernel(total, *refs):
    inputs = refs[:13]
    out = refs[13]
    loaded = refs[14:27]
    (
        d_ref,
        xe,
        dense,
        own_e,
        rows,
        got_e,
        got_m,
        got_2,
        got_3,
        back_1,
        back_2,
        back_3,
        gram_mine,
        gram_theirs,
        stats_mine,
        stats_theirs,
        near,
        a_mine,
        a_theirs,
        b_mine,
        b_theirs,
        w_mine,
        w_theirs,
        su_ref,
        su_got,
        stack,
        y_ref,
        y_main,
        a4_main,
        load_sem,
        send_sem,
        recv_sem,
        present,
    ) = refs[27:]
    signal, coverage = loaded[:2]
    codes, prior, levels, dead, base, wide, table_e, edge_cells, edge_first, edge_last, direct = loaded[2:]
    samples, length = signal.shape
    blocks = length // BLOCK
    chunks = length // CHUNK
    width = blocks * BLOCK + 128
    me = lax.axis_index("genome")
    peers = lax.axis_size("genome")
    side = lax.axis_index("sample")
    before = [lax.rem(me + peers - i, peers) for i in (1, 2, 3)]
    after = [lax.rem(me + i, peers) for i in (1, 2, 3)]

    barrier = pltpu.get_barrier_semaphore()
    for peer in before:
        pl.semaphore_signal(barrier, inc=1, device_id={"genome": peer})
    pl.semaphore_signal(barrier, inc=1, device_id={"sample": 1 - side})

    loads = {}

    def load(name, src, dst):
        c = pltpu.make_async_copy(src, dst, load_sem.at[len(loads)])
        c.start()
        loads[name] = c

    def load_chunk(i):
        span = pl.ds(i * CHUNK, CHUNK)
        load(("signal", i), inputs[0].at[:, span], signal.at[:, span])
        load(("coverage", i), inputs[1].at[:, span], coverage.at[:, span])

    names = ("codes", "prior", "levels", "dead", "base", "wide", "table_e", "cells", "first", "last", "direct")
    later = dict(zip(names, zip(inputs[2:], loaded[2:])))
    order = [chunks - 1, *range(chunks - 1)]
    load("base", *later["base"])
    load("codes", *later["codes"])
    load_chunk(order[0])
    load("last", *later["last"])
    load_chunk(order[1])
    load("first", *later["first"])
    for i in order[2:]:
        load_chunk(i)
    load("cells", *later["cells"])

    def copy(number, src, dst, device):
        return pltpu.make_async_remote_copy(
            src_ref=src,
            dst_ref=dst,
            send_sem=send_sem.at[number],
            recv_sem=recv_sem.at[number],
            device_id=device,
            device_id_type=pl.DeviceIdType.MESH,
        )

    loads["codes"].wait()
    d_ref[0:1, :] = jnp.ones((1, samples), F32)
    d_ref[1:8, :] = codes[...].astype(F32) - 2.0
    design = d_ref[...].astype(BF16)
    padded = jnp.concatenate([d_ref[...], jnp.zeros((120, samples), F32)], 0)
    gram_mine[...] = dot(design, padded.astype(BF16), NT)
    loads["base"].wait()
    for half in range(2):
        part = base[half].astype(F32)
        lane = lax.broadcasted_iota(jnp.int32, part.shape, 1)
        for b in range(blocks):
            moved = jnp.where(lane < 16, part, 0.0) if b == 0 else pltpu.roll(part, 16 * b, 1)
            dense[b * BLOCK : (b + 1) * BLOCK, half * 128 : half * 128 + 128] = moved.astype(BF16)

    def enter():
        pl.semaphore_wait(barrier, 4)
        for i, peer in enumerate(after):
            pl.semaphore_signal(present.at[i], inc=1, device_id={"genome": peer})

    def send_last():
        forward[0].start()
        gram_copy.start()

    forward = [copy(0, own_e, got_e, {"genome": after[0]})]
    gram_copy = copy(1, gram_mine, gram_theirs, {"sample": 1 - side})
    pl.when(me >= peers // 2)(enter)
    a4 = None
    for i in order:
        loads["signal", i].wait()
        loads["coverage", i].wait()
        span = slice(i * CHUNK, (i + 1) * CHUNK)
        x = (signal[:, span].astype(F32) * coverage[:, span].astype(F32)).astype(BF16)
        xe[:samples, span] = x
        if i == chunks - 1:
            loads["last"].wait()
            pair = dot(edge_last[...].reshape(64, TAIL), x, NT)
            own_e[...] = pair[:32] + pair[32:]
            pl.when(me >= peers // 2)(send_last)
        if i == 0:
            loads["first"].wait()
            pair = dot(edge_first[...].reshape(352, 128), x[:, :128], NT)
            first = pair[:176] + pair[176:]
        piece = dot(x, dense[span], NN)
        a4 = piece if a4 is None else a4 + piece
    a4 = halves(a4[:, :128] + a4[:, 128:])

    @pl.when(me < peers // 2)
    def _():
        enter()
        send_last()


    loads["cells"].wait()
    pair = dot(jnp.concatenate([edge_cells[0, 0:64], edge_cells[1, 0:64]], 0), a4[0], NT)
    rows[0:64] = pair[:64] + pair[64:] + dot(edge_cells[0, 0:64], a4[1], NT) + first[0:64]
    forward += [
        copy(2, rows.at[0:32], got_m, {"genome": after[0]}),
        copy(3, rows.at[32:48], got_2, {"genome": after[1]}),
        copy(4, rows.at[48:56], got_3, {"genome": after[2]}),
    ]
    for c in forward[1:]:
        c.start()
    for name in ("table_e", "wide", "prior", "levels", "dead", "direct"):
        load(name, *later[name])
    pair = dot(jnp.concatenate([edge_cells[0, 64:176], edge_cells[1, 64:176]], 0), a4[0], NT)
    rows[64:176] = pair[:112] + pair[112:] + dot(edge_cells[0, 64:176], a4[1], NT) + first[64:176]
    backward = [
        copy(6, rows.at[72:96], back_1, {"genome": before[0]}),
        copy(7, rows.at[96:112], back_2, {"genome": before[1]}),
        copy(8, rows.at[96:104], back_3, {"genome": before[2]}),
    ]
    near_copy = copy(12, rows.at[120:168], near, {"genome": before[0]})

    def send_backward():
        for i, c in enumerate(backward):
            pl.semaphore_wait(present.at[i], 1)
            c.start()

    pl.when(me > 0)(send_backward)

    for b in range(blocks):
        span = slice(b * BLOCK, (b + 1) * BLOCK)
        p = dot(design, xe[:samples, span], NN)
        high = p.astype(BF16).astype(F32)
        xe[samples:, span] = jnp.concatenate([high, p - high], 0).astype(BF16)

    gram_copy.wait()
    for name in ("prior", "levels", "dead"):
        loads[name].wait()
    lanes = lax.broadcasted_iota(jnp.int32, (8, 128), 1)
    subs = lax.broadcasted_iota(jnp.int32, (8, 128), 0)
    aug = gram_mine[...] + gram_theirs[...] + jnp.where(lanes == subs + 8, 1.0, 0.0)
    for k in range(DESIGN):
        row = aug[k : k + 1, :] / aug[k : k + 1, k : k + 1]
        aug = jnp.where(subs == k, row, aug - aug[:, k : k + 1] * row)
    diagonal = jnp.sum(jnp.where(lanes == subs + 8, aug, 0.0), 1, keepdims=True)
    inverse = [aug[:, 8 + k : 9 + k] for k in range(DESIGN)]
    weights = jnp.zeros(levels.shape, F32)
    for number in range(LEVELS + 1):
        weights = jnp.where(levels[...] == number, prior[number], weights)
    edge_weights = weights[:, BLOCK + 128 :]

    def shrink(m, s, weight):
        effects = inverse[0] * m[0:1]
        for k in range(1, DESIGN):
            effects = effects + inverse[k] * m[k : k + 1]
        left = jnp.sum(s, 0, keepdims=True) - jnp.sum(m * effects, 0, keepdims=True)
        noise = jnp.maximum(left, 0.0) / (total - DESIGN) + 1e-06
        squared = effects * effects
        return squared * effects / (squared + (noise * weight) * diagonal)

    def paired(shrunk):
        high = shrunk.astype(BF16).astype(F32)
        return jnp.concatenate([high, shrunk - high], 0).astype(BF16)

    def both(a, table, dims):
        return dot(a, table[0], dims) + dot(a, table[1], dims)

    def folded(res):
        return res[:8] + res[8:]

    def pick(a):
        return jnp.where(side == 0, a[:4], a[4:])

    only = jnp.where(lax.broadcasted_iota(jnp.int32, (8, 128), 0) == 0, 1.0, 0.0)
    only = only.astype(BF16)

    design2 = jnp.concatenate([design, design], 1)
    only2 = jnp.concatenate([only, only], 1)

    def summed(u, ref, skip=0):
        blank = [jnp.zeros((n, samples), F32) for n in (skip, 128 - skip - u.shape[0])]
        u = jnp.concatenate([*blank[:1], u, blank[1]] if skip else [u, blank[1]], 0)
        uh, ul = halves(u)
        squares = u * u
        sh, sl = halves(sum(squares[:, i : i + 128] for i in range(0, samples, 128)))
        ref[0:8] = dot(design2, jnp.concatenate([uh, ul], 1), NT)
        ref[8:16] = dot(only2, jnp.concatenate([sh, sl], 1), NT)

    def shrunk_edge(mine, theirs):
        total_edge = mine[...] + theirs[...]
        return shrink(total_edge[0:8], total_edge[8:16], edge_weights)

    a_copy = copy(9, a_mine, a_theirs, {"sample": 1 - side})
    b_copy = copy(10, b_mine, b_theirs, {"sample": 1 - side})
    su_copy = copy(11, su_ref, su_got, {"genome": before[0]})
    w_copy = copy(13, w_mine, w_theirs, {"sample": 1 - side})

    def u_before():
        return jnp.concatenate([rows[120:152] + got_e[...], rows[152:168] + got_m[0:16]], 0)

    def sum_before():
        forward[0].wait()
        forward[1].wait()
        summed(u_before(), a_mine)
        a_copy.start()

    def shrink_before():
        a_copy.wait()
        su_ref[...] = shrunk_edge(a_mine, a_theirs)

    def give_back():
        shrink_before()
        su_copy.start()

    pl.when(me == 1)(sum_before)
    for name in ("table_e", "wide"):
        loads[name].wait()
    spill = jnp.concatenate([wide[0, BLOCK:, 128:], wide[1, BLOCK:, 128:]], 1)
    e = dot3(a4, (table_e[0], table_e[1]), NN)
    eh, el = halves(e)
    stats_mine[0:8, width - 128 : width] = dot(design, eh, NN) + dot(design, el, NN)
    stats_mine[8:16, width - 128 : width] = jnp.sum((e * e).reshape(samples // 8, 8, 128), 0)
    for b in range(blocks):
        if b == 2:
            pl.when(me == 1)(give_back)
        depth = BLOCK + 128 if b < blocks - 1 else BLOCK
        span = slice(b * BLOCK, (b + 1) * BLOCK)
        window = xe[:, span]
        res = dot(window, wide[0, :BLOCK], NN) + dot(window, wide[1, :BLOCK], NN)
        if depth > BLOCK:
            tail = dot(xe[:, (b + 1) * BLOCK : b * BLOCK + depth], spill, NN)
            res = jnp.concatenate([res[:, :128], res[:, 128:] + tail[:, :128] + tail[:, 128:]], 1)
        main = res[:samples]
        stats_mine[0:8, span] = res[samples : samples + 8] + res[samples + 8 :]
        stats_mine[8:16, span] = jnp.sum((main * main).reshape(samples // 8, 8, BLOCK), 0)
    stats_copy = copy(5, stats_mine, stats_theirs, {"sample": 1 - side})
    stats_copy.start()

    pl.when(me > 1)(sum_before)

    @pl.when(me == 0)
    def _():
        send_backward()
        near_copy.start()


    stats_copy.wait()
    lane = lax.broadcasted_iota(jnp.int32, (8, BLOCK), 1)
    coarse = (lane >= 128) & (lane < 144)
    for b in range(blocks):
        span = slice(b * BLOCK, (b + 1) * BLOCK)
        m = stats_mine[0:8, span] + stats_theirs[0:8, span]
        s = stats_mine[8:16, span] + stats_theirs[8:16, span]
        g = jnp.where(coarse, 0.0, shrink(m, s, weights[:, :BLOCK]))
        if b == blocks - 1:
            g = jnp.where(dead[...] > 0, 0.0, g)
        stack[16 * b : 16 * b + 16, :] = paired(g)
    span = slice(width - 128, width)
    m = stats_mine[0:8, span] + stats_theirs[0:8, span]
    s = stats_mine[8:16, span] + stats_theirs[8:16, span]
    se = paired(shrink(m, s, weights[:, BLOCK : BLOCK + 128]))
    pl.when(me > 1)(give_back)

    y_main[...] = both(stack[...], (wide[0], wide[1]), NT)
    a4_main[...] = both(se, (table_e[0], table_e[1]), NT)

    a4 = folded(a4_main[...])
    narrow = lax.broadcasted_iota(jnp.int32, (8, 128), 1) < 16
    for b in range(blocks):
        moved = a4 if b == 0 else pltpu.roll(a4, 128 - 16 * b, 1)
        stack[16 * b : 16 * b + 16, :128] = paired(jnp.where(narrow, moved, 0.0))
    y = y_main[...] + both(stack[:, :128], (wide[0, :, 128:256], wide[1, :, 128:256]), NT)
    begin = jnp.zeros((8, 128), F32)
    for b in range(blocks):
        piece = folded(y[16 * b : 16 * b + 16])
        y_ref[:, b * BLOCK : b * BLOCK + 128] = pick(piece[:, :128] + begin)
        y_ref[:, b * BLOCK + 128 : (b + 1) * BLOCK] = pick(piece[:, 128:256])
        begin = piece[:, 256:]


    for c in backward + forward[2:]:
        c.wait()

    def u_long():
        u = rows[56:72] + got_m[16:32] + got_2[...] + back_1[0:16]
        return jnp.concatenate(
            [
                u[0:8] + back_2[0:8],
                u[8:16] + got_3[...],
                rows[112:120] + back_1[16:24] + back_2[8:16] + back_3[...],
            ],
            0,
        )

    @pl.when(me == 0)
    def _():
        forward[0].wait()
        forward[1].wait()
        summed(jnp.concatenate([u_before(), u_long()], 0), b_mine)
        su_ref[...] = jnp.zeros(su_ref.shape, F32)

    @pl.when(me > 0)
    def _():
        summed(u_long(), b_mine, 48)

    b_copy.start()

    @pl.when(me == peers - 1)
    def _():
        near_copy.wait_recv()
        summed(jnp.concatenate([own_e[...] + near[0:32], rows[0:16] + near[32:48]], 0), w_mine)
        w_copy.start()
        w_copy.wait()
        su_got[...] = shrunk_edge(w_mine, w_theirs)

    loads["direct"].wait()
    b_copy.wait()
    b_shrunk = shrunk_edge(b_mine, b_theirs)
    pl.when(me < peers - 1)(su_copy.wait_recv)
    su = pick(su_ref[...] + b_shrunk + pltpu.roll(su_got[...], 80, 1))
    last = both(paired(su), (direct[0], direct[1]), NN)
    out[...] = y_ref[...] + last[:4] + last[4:]
    pl.when(me > 0)(su_copy.wait_send)
    pl.when(me == 0)(near_copy.wait_send)


def local(signal, coverage, design_codes, level_prior):
    samples, length = signal.shape
    blocks = length // BLOCK
    *pairs, l_main, l_e, l_u, straddles = tables(length)
    pieces = [jnp.asarray(two(t)) for t in pairs]
    levels = jnp.asarray(np.concatenate([l_main, l_e, l_u])[None])
    dead = jnp.asarray(straddles.astype(np.int32)[None])
    total = samples * lax.axis_size("sample")
    width = blocks * BLOCK + 128
    operands = (signal, coverage, design_codes, level_prior, levels, dead, *pieces)
    places = [pltpu.VMEM(a.shape, a.dtype) for a in operands]
    places[3] = pltpu.SMEM(level_prior.shape, F32)
    copies = 14
    return pl.pallas_call(
        functools.partial(kernel, total),
        out_shape=pltpu.VMEM((DESIGN // lax.axis_size("sample"), length), F32),
        in_specs=[pl.BlockSpec(memory_space=pltpu.HBM)] * len(operands),
        out_specs=pl.BlockSpec(memory_space=pltpu.VMEM),
        scratch_shapes=places
        + [
            pltpu.VMEM((8, samples), F32),
            pltpu.VMEM((samples + 16, length), BF16),
            pltpu.VMEM((length, 256), BF16),
            pltpu.VMEM((32, samples), F32),
            pltpu.VMEM((176, samples), F32),
            pltpu.VMEM((32, samples), F32),
            pltpu.VMEM((32, samples), F32),
            pltpu.VMEM((16, samples), F32),
            pltpu.VMEM((8, samples), F32),
            pltpu.VMEM((24, samples), F32),
            pltpu.VMEM((16, samples), F32),
            pltpu.VMEM((8, samples), F32),
            pltpu.VMEM((8, 128), F32),
            pltpu.VMEM((8, 128), F32),
            pltpu.VMEM((16, width), F32),
            pltpu.VMEM((16, width), F32),
            pltpu.VMEM((48, samples), F32),
            pltpu.VMEM((16, 128), F32),
            pltpu.VMEM((16, 128), F32),
            pltpu.VMEM((16, 128), F32),
            pltpu.VMEM((16, 128), F32),
            pltpu.VMEM((16, 128), F32),
            pltpu.VMEM((16, 128), F32),
            pltpu.VMEM((8, 128), F32),
            pltpu.VMEM((8, 128), F32),
            pltpu.VMEM((16 * blocks, BLOCK), BF16),
            pltpu.VMEM((4, length), F32),
            pltpu.VMEM((16 * blocks, BLOCK + 128), F32),
            pltpu.VMEM((16, 128), F32),
            pltpu.SemaphoreType.DMA((11 + 2 * (length // CHUNK),)),
            pltpu.SemaphoreType.DMA((copies,)),
            pltpu.SemaphoreType.DMA((copies,)),
            pltpu.SemaphoreType.REGULAR((3,)),
        ],
        compiler_params=pltpu.CompilerParams(
            collective_id=0, has_side_effects=True, vmem_limit_bytes=56 * 2**20
        ),
    )(*operands)


def solution(mesh):
    placed = (
        P("sample", ("parts", "genome")),
        P("sample", ("parts", "genome")),
        P(None, "sample"),
        P(),
    )
    return jax.shard_map(
        local,
        mesh=mesh,
        in_specs=placed,
        out_specs=P("sample", ("parts", "genome")),
        check_vma=False,
    )
```

```python
import functools

import jax
import jax.numpy as jnp
import ml_dtypes
import numpy as np
from jax import lax
from jax.experimental import pallas as pl
from jax.experimental.pallas import tpu as pltpu
from jax.sharding import PartitionSpec as P

LEVELS = 10
DESIGN = 8
FINE = 4
BLOCK = 256
TAIL = 512
LOWPASS = np.array(
    (
        0.23037781330885523,
        0.7148465705525415,
        0.6308807679295904,
        -0.02798376941698385,
        -0.18703481171888114,
        0.030841381835986965,
        0.032883011666982945,
        -0.010597401784997278,
    )
)
HIGHPASS = np.array([(-1.0) ** m * LOWPASS[7 - m] for m in range(8)])


def spread(taps, step):
    out = np.zeros(7 * step + 1)
    out[::step] = taps
    return out


def composite(levels):
    low = np.ones(1)
    details = []
    for j in range(levels):
        details.append(np.convolve(low, spread(HIGHPASS, 2**j)))
        low = np.convolve(low, spread(LOWPASS, 2**j))
    return details, low


def column(taps, start, size):
    out = np.zeros(size)
    for i, tap in enumerate(taps):
        if 0 <= start + i < size:
            out[start + i] = tap
    return out


def tables(length):
    det, low = composite(LEVELS)
    fine_low = composite(FINE)[1]
    coarse_det, coarse_low = composite(LEVELS - FINE)
    cells = length >> FINE
    group1 = [(1, k) for k in range(125)] + [(2, k) for k in range(3)]
    group2 = [(0, k) for k in range(16)] + [(4, k) for k in range(16)] + [(3, k) for k in range(32)]
    group2 += [(2, k) for k in range(3, 64)] + [(1, k) for k in range(125, 128)]
    wide = np.zeros((BLOCK + 128, 2 * 128))
    level_main = np.zeros(256, np.int32)
    straddles = np.zeros(256, bool)
    for c, (level, k) in enumerate(group1 + group2):
        taps = det[level - 1] if level else fine_low
        step = 2 ** (level or FINE)
        wide[:, c] = column(taps, step * k, BLOCK + 128)
        level_main[c] = (level or 1) - 1
        straddles[c] = level > 0 and step * k + len(taps) > BLOCK
    coarse = [(level, k) for level in range(FINE + 1, LEVELS + 1) for k in range(length >> level)]
    coarse += [(0, k) for k in range(length >> LEVELS)]
    table_e = np.zeros((cells, 128))
    level_e = np.zeros(128, np.int32)
    for c, (level, k) in enumerate(coarse):
        taps = coarse_det[level - FINE - 1] if level else coarse_low
        step = 2 ** ((level or LEVELS) - FINE)
        level_e[c] = level - 1 if level else LEVELS
        full = det[level - 1] if level else low
        if (step << FINE) * k + len(full) <= length:
            table_e[:, c] = column(taps, step * k, cells)
    edge = []
    for level in range(1, LEVELS + 1):
        size = length >> level
        first = -(-(length - len(det[level - 1]) + 1) // 2**level)
        edge += [(level, k) for k in range(max(first, 0), size)]
    early = [e for e in edge if e[0] < 7]
    middle = [e for e in edge if 7 <= e[0] < 9 or (e[0] == 9 and e[1] < 2)]
    late = [e for e in edge if e not in early + middle] + [(0, k) for k in range(length >> LEVELS)]
    early += [None] * (32 - len(early))
    middle += [None] * (16 - len(middle))
    late += [None] * (8 - len(late))
    coarsest = late[2:6]
    none = [None] * 2
    sets = [row for row in late if row]
    levels = np.zeros(128, np.int32)
    for r, row in enumerate(early + middle + sets + sets + coarsest + late):
        if row:
            levels[r] = row[0] - 1 if row[0] else LEVELS
    shifted = []
    for shift, part in (
        (0, middle + sets), (1, sets), (2, coarsest),
        (0, 3 * none + sets), (1, coarsest),
        (0, 2 * none + coarsest),
        (1, sets), (2, sets), (3, coarsest),
        (2, sets), (3, sets), (0, 2 * none), (1, late),
        (3, late), (2, late),
        (0, late),
        (1, early + middle),
    ):
        shifted += [(row, shift * length) for row in part]
    edge_cells = np.zeros((176, cells))
    edge_first = np.zeros((176, 128))
    edge_last = np.zeros((32, TAIL))
    direct = np.zeros((128, length))
    into = {**{120 + r: r for r in range(48)}, **{56 + r: 48 + r for r in range(16)}, **{112 + r: 64 + r for r in range(8)}}
    for r, (row, shift) in enumerate(shifted):
        if row is None:
            continue
        level, k = row
        if r in into:
            full = det[level - 1] if level else low
            direct[into[r]] = column(full, k * 2 ** (level or LEVELS) - shift, length)
        if 1 <= level <= FINE:
            edge_first[r] = column(det[level - 1], k * 2**level - shift, 128)
            continue
        taps = coarse_det[level - FINE - 1] if level else coarse_low
        start = k * 2 ** ((level or LEVELS) - FINE) - (shift >> FINE)
        edge_cells[r] = column(taps, start, cells)
        for c in range(-6, 0):
            if 0 <= c - start < len(taps):
                edge_first[r] += taps[c - start] * column(fine_low, c * 2**FINE, 128)
    for r, row in enumerate(early + middle):
        if row:
            direct[80 + r] = column(det[row[0] - 1], row[1] * 2 ** row[0], length)
    for r, row in enumerate(early):
        if row:
            edge_last[r] = column(det[row[0] - 1], row[1] * 2 ** row[0] - (length - TAIL), TAIL)
    base = np.stack([column(fine_low, (k if k < 16 else k - 128) * 2**FINE, BLOCK) for k in range(128)], 1)
    return base, wide, table_e, edge_cells, edge_first, edge_last, direct, level_main, level_e, levels, straddles


def two(table):
    high = table.astype(np.float32).astype(ml_dtypes.bfloat16)
    rest = (table - high.astype(np.float64)).astype(np.float32).astype(ml_dtypes.bfloat16)
    return np.stack([high, rest])


NN = (((1,), (0,)), ((), ()))
NT = (((1,), (1,)), ((), ()))


def dot(a, b, dims):
    return lax.dot_general(a, b, dims, preferred_element_type=jnp.float32)


def halves(a):
    high = a.astype(jnp.bfloat16)
    return high, (a - high.astype(jnp.float32)).astype(jnp.bfloat16)


def dot3(a, b, dims):
    return dot(a[0], b[0], dims) + dot(a[0], b[1], dims) + dot(a[1], b[0], dims)


CHUNK = 512
F32 = jnp.float32
BF16 = jnp.bfloat16


def kernel(total, *refs):
    inputs = refs[:13]
    out = refs[13]
    loaded = refs[14:27]
    (
        d_ref,
        xe,
        dense,
        own_e,
        rows,
        got_e,
        got_m,
        got_2,
        got_3,
        back_1,
        back_2,
        back_3,
        gram_mine,
        gram_theirs,
        stats_mine,
        stats_theirs,
        near,
        a_mine,
        a_theirs,
        b_mine,
        b_theirs,
        w_mine,
        w_theirs,
        su_ref,
        su_got,
        stack,
        y_ref,
        y_main,
        a4_main,
        load_sem,
        send_sem,
        recv_sem,
        present,
    ) = refs[27:]
    signal, coverage = loaded[:2]
    codes, prior, levels, dead, base, wide, table_e, edge_cells, edge_first, edge_last, direct = loaded[2:]
    samples, length = signal.shape
    blocks = length // BLOCK
    chunks = length // CHUNK
    width = blocks * BLOCK + 128
    me = lax.axis_index("genome")
    peers = lax.axis_size("genome")
    side = lax.axis_index("sample")
    before = [lax.rem(me + peers - i, peers) for i in (1, 2, 3)]
    after = [lax.rem(me + i, peers) for i in (1, 2, 3)]

    barrier = pltpu.get_barrier_semaphore()
    for peer in before:
        pl.semaphore_signal(barrier, inc=1, device_id={"genome": peer})
    pl.semaphore_signal(barrier, inc=1, device_id={"sample": 1 - side})

    loads = {}

    def load(name, src, dst):
        c = pltpu.make_async_copy(src, dst, load_sem.at[len(loads)])
        c.start()
        loads[name] = c

    def load_chunk(i):
        span = pl.ds(i * CHUNK, CHUNK)
        load(("signal", i), inputs[0].at[:, span], signal.at[:, span])
        load(("coverage", i), inputs[1].at[:, span], coverage.at[:, span])

    names = ("codes", "prior", "levels", "dead", "base", "wide", "table_e", "cells", "first", "last", "direct")
    later = dict(zip(names, zip(inputs[2:], loaded[2:])))
    order = [chunks - 1, *range(chunks - 1)]
    load("base", *later["base"])
    load("codes", *later["codes"])
    load_chunk(order[0])
    load("last", *later["last"])
    load_chunk(order[1])
    load("first", *later["first"])
    for i in order[2:]:
        load_chunk(i)
    load("cells", *later["cells"])

    def copy(number, src, dst, device):
        return pltpu.make_async_remote_copy(
            src_ref=src,
            dst_ref=dst,
            send_sem=send_sem.at[number],
            recv_sem=recv_sem.at[number],
            device_id=device,
            device_id_type=pl.DeviceIdType.MESH,
        )

    loads["codes"].wait()
    d_ref[0:1, :] = jnp.ones((1, samples), F32)
    d_ref[1:8, :] = codes[...].astype(F32) - 2.0
    design = d_ref[...].astype(BF16)
    padded = jnp.concatenate([d_ref[...], jnp.zeros((120, samples), F32)], 0)
    gram_mine[...] = dot(design, padded.astype(BF16), NT)
    loads["base"].wait()
    for half in range(2):
        part = base[half].astype(F32)
        lane = lax.broadcasted_iota(jnp.int32, part.shape, 1)
        for b in range(blocks):
            moved = jnp.where(lane < 16, part, 0.0) if b == 0 else pltpu.roll(part, 16 * b, 1)
            dense[b * BLOCK : (b + 1) * BLOCK, half * 128 : half * 128 + 128] = moved.astype(BF16)

    def enter():
        pl.semaphore_wait(barrier, 4)
        for i, peer in enumerate(after):
            pl.semaphore_signal(present.at[i], inc=1, device_id={"genome": peer})

    def send_last():
        forward[0].start()
        gram_copy.start()

    forward = [copy(0, own_e, got_e, {"genome": after[0]})]
    gram_copy = copy(1, gram_mine, gram_theirs, {"sample": 1 - side})
    pl.when(me >= peers // 2)(enter)
    a4 = None
    for i in order:
        loads["signal", i].wait()
        loads["coverage", i].wait()
        span = slice(i * CHUNK, (i + 1) * CHUNK)
        x = (signal[:, span].astype(F32) * coverage[:, span].astype(F32)).astype(BF16)
        xe[:samples, span] = x
        if i == chunks - 1:
            loads["last"].wait()
            pair = dot(edge_last[...].reshape(64, TAIL), x, NT)
            own_e[...] = pair[:32] + pair[32:]
            pl.when(me >= peers // 2)(send_last)
        if i == 0:
            loads["first"].wait()
            pair = dot(edge_first[...].reshape(352, 128), x[:, :128], NT)
            first = pair[:176] + pair[176:]
        piece = dot(x, dense[span], NN)
        a4 = piece if a4 is None else a4 + piece
    a4 = halves(a4[:, :128] + a4[:, 128:])

    @pl.when(me < peers // 2)
    def _():
        enter()
        send_last()


    loads["cells"].wait()
    pair = dot(jnp.concatenate([edge_cells[0, 0:64], edge_cells[1, 0:64]], 0), a4[0], NT)
    rows[0:64] = pair[:64] + pair[64:] + dot(edge_cells[0, 0:64], a4[1], NT) + first[0:64]
    forward += [
        copy(2, rows.at[0:32], got_m, {"genome": after[0]}),
        copy(3, rows.at[32:48], got_2, {"genome": after[1]}),
        copy(4, rows.at[48:56], got_3, {"genome": after[2]}),
    ]
    forward[1].start()
    for name in ("table_e", "wide", "prior", "levels", "dead", "direct"):
        load(name, *later[name])
    pair = dot(jnp.concatenate([edge_cells[0, 64:176], edge_cells[1, 64:176]], 0), a4[0], NT)
    rows[64:176] = pair[:112] + pair[112:] + dot(edge_cells[0, 64:176], a4[1], NT) + first[64:176]
    backward = [
        copy(6, rows.at[72:96], back_1, {"genome": before[0]}),
        copy(7, rows.at[96:112], back_2, {"genome": before[1]}),
        copy(8, rows.at[96:104], back_3, {"genome": before[2]}),
    ]
    near_copy = copy(12, rows.at[120:168], near, {"genome": before[0]})

    def send_backward():
        for i, c in enumerate(backward):
            pl.semaphore_wait(present.at[i], 1)
            c.start()

    for c in forward[2:]:
        c.start()
    pl.when(me > 0)(send_backward)

    for b in range(blocks):
        span = slice(b * BLOCK, (b + 1) * BLOCK)
        p = dot(design, xe[:samples, span], NN)
        high = p.astype(BF16).astype(F32)
        xe[samples:, span] = jnp.concatenate([high, p - high], 0).astype(BF16)

    gram_copy.wait()
    for name in ("prior", "levels", "dead"):
        loads[name].wait()
    lanes = lax.broadcasted_iota(jnp.int32, (8, 128), 1)
    subs = lax.broadcasted_iota(jnp.int32, (8, 128), 0)
    aug = gram_mine[...] + gram_theirs[...] + jnp.where(lanes == subs + 8, 1.0, 0.0)
    for k in range(DESIGN):
        row = aug[k : k + 1, :] / aug[k : k + 1, k : k + 1]
        aug = jnp.where(subs == k, row, aug - aug[:, k : k + 1] * row)
    diagonal = jnp.sum(jnp.where(lanes == subs + 8, aug, 0.0), 1, keepdims=True)
    inverse = [aug[:, 8 + k : 9 + k] for k in range(DESIGN)]
    weights = jnp.zeros(levels.shape, F32)
    for number in range(LEVELS + 1):
        weights = jnp.where(levels[...] == number, prior[number], weights)
    edge_weights = weights[:, BLOCK + 128 :]

    def shrink(m, s, weight):
        effects = inverse[0] * m[0:1]
        for k in range(1, DESIGN):
            effects = effects + inverse[k] * m[k : k + 1]
        left = jnp.sum(s, 0, keepdims=True) - jnp.sum(m * effects, 0, keepdims=True)
        noise = jnp.maximum(left, 0.0) / (total - DESIGN) + 1e-06
        squared = effects * effects
        return squared * effects / (squared + (noise * weight) * diagonal)

    def paired(shrunk):
        high = shrunk.astype(BF16).astype(F32)
        return jnp.concatenate([high, shrunk - high], 0).astype(BF16)

    def both(a, table, dims):
        return dot(a, table[0], dims) + dot(a, table[1], dims)

    def folded(res):
        return res[:8] + res[8:]

    def pick(a):
        return jnp.where(side == 0, a[:4], a[4:])

    only = jnp.where(lax.broadcasted_iota(jnp.int32, (8, 128), 0) == 0, 1.0, 0.0)
    only = only.astype(BF16)

    design2 = jnp.concatenate([design, design], 1)
    only2 = jnp.concatenate([only, only], 1)

    def summed(u, ref, skip=0):
        blank = [jnp.zeros((n, samples), F32) for n in (skip, 128 - skip - u.shape[0])]
        u = jnp.concatenate([*blank[:1], u, blank[1]] if skip else [u, blank[1]], 0)
        uh, ul = halves(u)
        squares = u * u
        sh, sl = halves(sum(squares[:, i : i + 128] for i in range(0, samples, 128)))
        ref[0:8] = dot(design2, jnp.concatenate([uh, ul], 1), NT)
        ref[8:16] = dot(only2, jnp.concatenate([sh, sl], 1), NT)

    def shrunk_edge(mine, theirs):
        total_edge = mine[...] + theirs[...]
        return shrink(total_edge[0:8], total_edge[8:16], edge_weights)

    a_copy = copy(9, a_mine, a_theirs, {"sample": 1 - side})
    b_copy = copy(10, b_mine, b_theirs, {"sample": 1 - side})
    su_copy = copy(11, su_ref, su_got, {"genome": before[0]})
    w_copy = copy(13, w_mine, w_theirs, {"sample": 1 - side})

    def u_before():
        return jnp.concatenate([rows[120:152] + got_e[...], rows[152:168] + got_m[0:16]], 0)

    def sum_before():
        forward[0].wait()
        forward[1].wait()
        summed(u_before(), a_mine)
        a_copy.start()

    def shrink_before():
        a_copy.wait()
        su_ref[...] = shrunk_edge(a_mine, a_theirs)

    def give_back():
        shrink_before()
        su_copy.start()

    pl.when(me == 1)(sum_before)
    for name in ("table_e", "wide"):
        loads[name].wait()
    spill = jnp.concatenate([wide[0, BLOCK:, 128:], wide[1, BLOCK:, 128:]], 1)
    e = dot3(a4, (table_e[0], table_e[1]), NN)
    eh, el = halves(e)
    stats_mine[0:8, width - 128 : width] = dot(design, eh, NN) + dot(design, el, NN)
    stats_mine[8:16, width - 128 : width] = jnp.sum((e * e).reshape(samples // 8, 8, 128), 0)
    for b in range(blocks):
        if b == 2:
            pl.when(me == 1)(give_back)
        depth = BLOCK + 128 if b < blocks - 1 else BLOCK
        span = slice(b * BLOCK, (b + 1) * BLOCK)
        window = xe[:, span]
        res = dot(window, wide[0, :BLOCK], NN) + dot(window, wide[1, :BLOCK], NN)
        if depth > BLOCK:
            tail = dot(xe[:, (b + 1) * BLOCK : b * BLOCK + depth], spill, NN)
            res = jnp.concatenate([res[:, :128], res[:, 128:] + tail[:, :128] + tail[:, 128:]], 1)
        main = res[:samples]
        stats_mine[0:8, span] = res[samples : samples + 8] + res[samples + 8 :]
        stats_mine[8:16, span] = jnp.sum((main * main).reshape(samples // 8, 8, BLOCK), 0)
    stats_copy = copy(5, stats_mine, stats_theirs, {"sample": 1 - side})
    stats_copy.start()

    pl.when(me > 1)(sum_before)

    @pl.when(me == 0)
    def _():
        send_backward()
        near_copy.start()


    stats_copy.wait()
    lane = lax.broadcasted_iota(jnp.int32, (8, BLOCK), 1)
    coarse = (lane >= 128) & (lane < 144)
    for b in range(blocks):
        span = slice(b * BLOCK, (b + 1) * BLOCK)
        m = stats_mine[0:8, span] + stats_theirs[0:8, span]
        s = stats_mine[8:16, span] + stats_theirs[8:16, span]
        g = jnp.where(coarse, 0.0, shrink(m, s, weights[:, :BLOCK]))
        if b == blocks - 1:
            g = jnp.where(dead[...] > 0, 0.0, g)
        stack[16 * b : 16 * b + 16, :] = paired(g)
    span = slice(width - 128, width)
    m = stats_mine[0:8, span] + stats_theirs[0:8, span]
    s = stats_mine[8:16, span] + stats_theirs[8:16, span]
    se = paired(shrink(m, s, weights[:, BLOCK : BLOCK + 128]))
    pl.when(me > 1)(give_back)

    y_main[...] = both(stack[...], (wide[0], wide[1]), NT)
    a4_main[...] = both(se, (table_e[0], table_e[1]), NT)

    a4 = folded(a4_main[...])
    narrow = lax.broadcasted_iota(jnp.int32, (8, 128), 1) < 16
    for b in range(blocks):
        moved = a4 if b == 0 else pltpu.roll(a4, 128 - 16 * b, 1)
        stack[16 * b : 16 * b + 16, :128] = paired(jnp.where(narrow, moved, 0.0))
    y = y_main[...] + both(stack[:, :128], (wide[0, :, 128:256], wide[1, :, 128:256]), NT)
    begin = jnp.zeros((8, 128), F32)
    for b in range(blocks):
        piece = folded(y[16 * b : 16 * b + 16])
        y_ref[:, b * BLOCK : b * BLOCK + 128] = pick(piece[:, :128] + begin)
        y_ref[:, b * BLOCK + 128 : (b + 1) * BLOCK] = pick(piece[:, 128:256])
        begin = piece[:, 256:]


    for c in backward + forward[2:]:
        c.wait()

    def u_long():
        u = rows[56:72] + got_m[16:32] + got_2[...] + back_1[0:16]
        return jnp.concatenate(
            [
                u[0:8] + back_2[0:8],
                u[8:16] + got_3[...],
                rows[112:120] + back_1[16:24] + back_2[8:16] + back_3[...],
            ],
            0,
        )

    @pl.when(me == 0)
    def _():
        forward[0].wait()
        forward[1].wait()
        summed(jnp.concatenate([u_before(), u_long()], 0), b_mine)
        su_ref[...] = jnp.zeros(su_ref.shape, F32)

    @pl.when(me > 0)
    def _():
        summed(u_long(), b_mine, 48)

    b_copy.start()

    @pl.when(me == peers - 1)
    def _():
        near_copy.wait_recv()
        summed(jnp.concatenate([own_e[...] + near[0:32], rows[0:16] + near[32:48]], 0), w_mine)
        w_copy.start()
        w_copy.wait()
        su_got[...] = shrunk_edge(w_mine, w_theirs)

    loads["direct"].wait()
    b_copy.wait()
    b_shrunk = shrunk_edge(b_mine, b_theirs)
    pl.when(me < peers - 1)(su_copy.wait_recv)
    su = pick(su_ref[...] + b_shrunk + pltpu.roll(su_got[...], 80, 1))
    last = both(paired(su), (direct[0], direct[1]), NN)
    out[...] = y_ref[...] + last[:4] + last[4:]
    pl.when(me > 0)(su_copy.wait_send)
    pl.when(me == 0)(near_copy.wait_send)


def local(signal, coverage, design_codes, level_prior):
    samples, length = signal.shape
    blocks = length // BLOCK
    *pairs, l_main, l_e, l_u, straddles = tables(length)
    pieces = [jnp.asarray(two(t)) for t in pairs]
    levels = jnp.asarray(np.concatenate([l_main, l_e, l_u])[None])
    dead = jnp.asarray(straddles.astype(np.int32)[None])
    total = samples * lax.axis_size("sample")
    width = blocks * BLOCK + 128
    operands = (signal, coverage, design_codes, level_prior, levels, dead, *pieces)
    places = [pltpu.VMEM(a.shape, a.dtype) for a in operands]
    places[3] = pltpu.SMEM(level_prior.shape, F32)
    copies = 14
    return pl.pallas_call(
        functools.partial(kernel, total),
        out_shape=pltpu.VMEM((DESIGN // lax.axis_size("sample"), length), F32),
        in_specs=[pl.BlockSpec(memory_space=pltpu.HBM)] * len(operands),
        out_specs=pl.BlockSpec(memory_space=pltpu.VMEM),
        scratch_shapes=places
        + [
            pltpu.VMEM((8, samples), F32),
            pltpu.VMEM((samples + 16, length), BF16),
            pltpu.VMEM((length, 256), BF16),
            pltpu.VMEM((32, samples), F32),
            pltpu.VMEM((176, samples), F32),
            pltpu.VMEM((32, samples), F32),
            pltpu.VMEM((32, samples), F32),
            pltpu.VMEM((16, samples), F32),
            pltpu.VMEM((8, samples), F32),
            pltpu.VMEM((24, samples), F32),
            pltpu.VMEM((16, samples), F32),
            pltpu.VMEM((8, samples), F32),
            pltpu.VMEM((8, 128), F32),
            pltpu.VMEM((8, 128), F32),
            pltpu.VMEM((16, width), F32),
            pltpu.VMEM((16, width), F32),
            pltpu.VMEM((48, samples), F32),
            pltpu.VMEM((16, 128), F32),
            pltpu.VMEM((16, 128), F32),
            pltpu.VMEM((16, 128), F32),
            pltpu.VMEM((16, 128), F32),
            pltpu.VMEM((16, 128), F32),
            pltpu.VMEM((16, 128), F32),
            pltpu.VMEM((8, 128), F32),
            pltpu.VMEM((8, 128), F32),
            pltpu.VMEM((16 * blocks, BLOCK), BF16),
            pltpu.VMEM((4, length), F32),
            pltpu.VMEM((16 * blocks, BLOCK + 128), F32),
            pltpu.VMEM((16, 128), F32),
            pltpu.SemaphoreType.DMA((11 + 2 * (length // CHUNK),)),
            pltpu.SemaphoreType.DMA((copies,)),
            pltpu.SemaphoreType.DMA((copies,)),
            pltpu.SemaphoreType.REGULAR((3,)),
        ],
        compiler_params=pltpu.CompilerParams(
            collective_id=0, has_side_effects=True, vmem_limit_bytes=56 * 2**20
        ),
    )(*operands)


def solution(mesh):
    placed = (
        P("sample", ("parts", "genome")),
        P("sample", ("parts", "genome")),
        P(None, "sample"),
        P(),
    )
    return jax.shard_map(
        local,
        mesh=mesh,
        in_specs=placed,
        out_specs=P("sample", ("parts", "genome")),
        check_vma=False,
    )
```
